32 devices in a mesh: tm: 8 (over z, x), height: 2 (over y), width: 2 (over core).
Axes of the slice: x: 2, y: 2, z: 4, core: 2. Of those that a mesh axis runs over, the one named last changes fastest.
Arguments:
- features: bfloat16 [32, 32, 64, 128], P('tm', 'height', 'width'), may hold values from -6 to 6
- grad_out: bfloat16 [32, 32, 64, 128], P('tm', 'height', 'width'), may hold values from -60 to 60
- mean_saved: float32 [32, 32], P('tm'), may hold values from -3 to 3
- rstd_saved: float32 [32, 32], P('tm'), may hold values from 0.5 to 2
- gain: float32 [128], replicated, may hold values from 0.5 to 1.5
- bias: float32 [128], replicated, may hold values from -3 to 3
- weight: bfloat16 [3, 3, 3, 128, 128], replicated, may hold values from -0.109375 to 0.109375
- future_cot: bfloat16 [2, 32, 64, 128], P(None, 'height', 'width'), may hold values from -6 to 6
Outputs:
- input_cot: bfloat16 [32, 32, 64, 128], P('tm', 'height', 'width')
- weight_grad: float32 [3456, 128], P('tm')
The draws below stay inside these ranges and needn't reach their ends.
All inputs are finite; a program needn't handle non-finite values.
Results may differ from the reference program's by a relative error of at most 0.003.
Values may be sent and summed in bfloat16 or wider, within the bound.
No kernel may reach another device: no remote copies, remote signals or barrier semaphores. Data moves between devices by JAX's collectives and lax.ppermute only.
A program may use at most 64 MiB of HBM per device.

```python
import math
import jax
import jax.numpy as jnp
from jax import lax

C = 128
G = 32
TF = 32
NH = 32
NW = 64


def draw_grad_out(key, part):
    key_base, key_rows = jax.random.split(key)
    row_pos = jnp.arange(NH, dtype=jnp.float32) / NH
    col_pos = jnp.arange(NW, dtype=jnp.float32) / NW
    position = jnp.power(3.0, row_pos[:, None] + col_pos[None, :])
    row_factor = jnp.exp(jax.random.uniform(key_rows, (TF, NH, 1, 1), jnp.float32, math.log(0.3), math.log(1.1)))
    base = jnp.clip(jax.random.normal(key_base, (TF, NH, NW, C), jnp.float32), -6.0, 6.0)
    values = base * position[None, :, :, None] * row_factor
    return values.astype(jnp.bfloat16)


def level_of(rng, extent, pieces, least, largest):
    level = 1.0
    for dim, parts in pieces:
        steps = jax.random.uniform(jax.random.fold_in(jax.random.fold_in(rng, 6), dim), (parts,), jnp.float32, least / len(pieces), largest / len(pieces))
        level = level * jnp.repeat(jnp.exp(steps), extent[dim] // parts).reshape((-1,) + (1,) * (len(extent) - 1 - dim))
    return level


def normal_values(own_key, shape, width, limit, shards=(), kind=jnp.bfloat16):
    values = width * jax.random.normal(own_key, shape, jnp.float32)
    if shards:
        values = values * level_of(own_key, shape, shards, -0.22, 0.18)
    return jnp.clip(values, -limit, limit).astype(kind)


def setup_inputs(seed: int = 0) -> dict:
    arg_keys = jax.random.split(jax.random.key(seed), 9)
    return {
        "features": normal_values(arg_keys[0], (TF, NH, NW, C), 1.0, 6.0, ((0, 8), (1, 2), (2, 2))),
        "grad_out": draw_grad_out(jax.random.fold_in(arg_keys[8], 71), 0),
        "mean_saved": normal_values(arg_keys[2], (TF, G), 0.5, 3.0, ((0, 8),), jnp.float32),
        "rstd_saved": jnp.clip(jnp.exp(math.log(2.0) - 1.3862944 * jax.random.uniform(arg_keys[3], (TF, G), jnp.float32) ** level_of(arg_keys[3], (TF, G), ((0, 8),), -0.2, 0.2)), 0.5, 2.0),
        "gain": jnp.clip(1.0 + 0.1 * jax.random.normal(arg_keys[4], (C,), jnp.float32), 0.5, 1.5),
        "bias": normal_values(arg_keys[5], (C,), 0.5, 3.0, (), jnp.float32),
        "weight": normal_values(arg_keys[6], (3, 3, 3, C, C), (27 * C) ** -0.5, 0.109375),
        "future_cot": normal_values(arg_keys[7], (2, NH, NW, C), 1.0, 6.0, ((1, 2), (2, 2))),
    }


def reference(features, grad_out, mean_saved, rstd_saved, gain, bias, weight, future_cot):
    total_frames, height_cells, width_cells, channels = features.shape
    groups = mean_saved.shape[1]
    group_width = channels // groups
    grouped_in = features.astype(jnp.float32).reshape(total_frames, height_cells, width_cells, groups, group_width)
    centred = (grouped_in - mean_saved[:, None, None, :, None]) * rstd_saved[:, None, None, :, None]
    normed = centred.reshape(total_frames, height_cells, width_cells, channels)
    pre_act = normed * gain + bias
    sigmoid_val = jax.nn.sigmoid(pre_act)
    activation = (pre_act * sigmoid_val).astype(jnp.bfloat16)
    flat_act = activation.reshape(-1, channels)
    padded = jnp.pad(grad_out, ((0, 2), (1, 1), (1, 1), (0, 0)))
    act_cot = jnp.zeros((flat_act.shape[0], channels), jnp.float32)
    blocks = []
    for lag_t in range(3):
        for lag_h in range(3):
            for lag_w in range(3):
                window = padded[2 - lag_t:2 - lag_t + total_frames, 2 - lag_h:2 - lag_h + height_cells, 2 - lag_w:2 - lag_w + width_cells].reshape(-1, channels)
                act_cot = act_cot + lax.dot_general(window, weight[lag_t, lag_h, lag_w], (((1,), (1,)), ((), ())), preferred_element_type=jnp.float32)
                blocks.append(lax.dot_general(flat_act, window, (((0,), (0,)), ((), ())), preferred_element_type=jnp.float32))
    act_cot = act_cot.reshape(total_frames, height_cells, width_cells, channels)
    act_cot = jnp.concatenate([act_cot[:total_frames - 2], act_cot[total_frames - 2:] + future_cot.astype(jnp.float32)], axis=0)
    scaled = act_cot * sigmoid_val * (1.0 + pre_act * (1.0 - sigmoid_val)) * gain
    scaled_groups = scaled.reshape(total_frames, height_cells, width_cells, groups, group_width)
    count = height_cells * width_cells * group_width
    first = lax.optimization_barrier(jnp.sum(scaled_groups, axis=(1, 2, 4))) / count
    second = lax.optimization_barrier(jnp.sum(scaled_groups * centred, axis=(1, 2, 4))) / count
    corrected = rstd_saved[:, None, None, :, None] * (scaled_groups - first[:, None, None, :, None] - centred * second[:, None, None, :, None])
    input_cot = (grad_out.astype(jnp.float32) + corrected.reshape(total_frames, height_cells, width_cells, channels)).astype(jnp.bfloat16)
    grad_scale = 1.0 / math.sqrt(total_frames * height_cells * width_cells)
    weight_grad = jnp.stack(blocks).reshape(27 * channels, channels) * grad_scale
    return (input_cot, weight_grad)
```

```python
import math

import jax
import jax.numpy as jnp
from jax import lax
from jax.sharding import PartitionSpec as P


def extended_2(cells, sides, width):
    for axis, dim in sides:
        count = lax.axis_size(axis)
        ends = count - 1
        head = lax.slice_in_dim(cells, 0, width, axis=dim)
        tail = lax.slice_in_dim(cells, cells.shape[dim] - width, cells.shape[dim], axis=dim)
        cells = jnp.concatenate(
            [
                lax.ppermute(tail, axis, [(i, (i + 1) % count) for i in range(ends)]),
                cells,
                lax.ppermute(head, axis, [((i + 1) % count, i) for i in range(ends)]),
            ],
            axis=dim,
        )
    return cells


def shifted(value, axis, steps):
    count = lax.axis_size(axis)
    initial, last = (max(0, -steps), min(count, count - steps))
    return lax.ppermute(value, axis, [(source, source + steps) for source in range(initial, last)])


def exchanged(value, axis, distance):
    count = lax.axis_size(axis)
    return lax.ppermute(value, axis, [(i, i ^ distance) for i in range(count)])


def kept_rows(rows):
    return -(-rows // 16) * 8


def halved(value, axis, wire):
    rows = value.shape[1]
    kept = kept_rows(rows)
    index = lax.axis_index(axis)
    mine = lax.dynamic_slice_in_dim(value, index * (rows - kept), kept, 1)
    theirs = lax.dynamic_slice_in_dim(value, (1 - index) * (rows - kept), kept, 1)
    return mine + exchanged(theirs.astype(wire), axis, 1).astype(jnp.float32)


def joined(low, high, rows):
    kept = low.shape[0]
    return jnp.concatenate([low, high[2 * kept - rows :]], axis=0)


def power_of_two(count):
    return count & (count - 1) == 0


def reduced_share(partial):
    rows_all, channels = partial.shape
    blocks = lax.axis_size("tm")
    rows = rows_all // blocks
    pairs = lax.axis_size("height") == 2 and lax.axis_size("width") == 2
    if not (pairs and power_of_two(blocks) and rows % 8 == 0):
        share = lax.psum_scatter(partial, "tm", scatter_dimension=0, tiled=True)
        return lax.psum(share, ("height", "width"))
    value = partial.reshape(blocks, rows, channels)
    value = halved(value, "width", jnp.float32)
    half = value.shape[1]
    value = halved(value, "height", jnp.bfloat16)
    place = lax.axis_index("tm")
    distance = 1
    while distance < blocks:
        side = (place // distance) % 2
        split = value.reshape(value.shape[0] // 2, 2, *value.shape[1:])
        mine = lax.dynamic_index_in_dim(split, side, 1, keepdims=False)
        theirs = lax.dynamic_index_in_dim(split, 1 - side, 1, keepdims=False)
        wire = jnp.float32 if split.shape[0] == 1 else jnp.bfloat16
        value = mine + exchanged(theirs.astype(wire), "tm", distance).astype(jnp.float32)
        distance *= 2
    own = value[0]
    beside = exchanged(own, "width", 1)
    below = exchanged(own, "height", 1)
    across = lax.ppermute(own, ("height", "width"), [(i, 3 - i) for i in range(4)])
    row_side = lax.axis_index("height")
    col_side = lax.axis_index("width")
    mine_half = joined(
        jnp.where(row_side == 0, own, below), jnp.where(row_side == 0, below, own), half
    )
    other_half = joined(
        jnp.where(row_side == 0, beside, across), jnp.where(row_side == 0, across, beside), half
    )
    return joined(
        jnp.where(col_side == 0, mine_half, other_half),
        jnp.where(col_side == 0, other_half, mine_half),
        rows,
    )


def on_device(features, grad_out, mean_saved, rstd_saved, gain, bias, weight, future_cot):
    frame_count, row_count, col_count, channels = features.shape
    groups = mean_saved.shape[1]
    group_width = channels // groups
    grouped_in = features.astype(jnp.float32).reshape(
        frame_count, row_count, col_count, groups, group_width
    )
    centred = (grouped_in - mean_saved[:, None, None, :, None]) * rstd_saved[:, None, None, :, None]
    normed = centred.reshape(frame_count, row_count, col_count, channels)
    pre_act = normed * gain + bias
    sigmoid_val = jax.nn.sigmoid(pre_act)
    activation = (pre_act * sigmoid_val).astype(jnp.bfloat16)
    flat_act = activation.reshape(-1, channels)
    padded = extended_2(grad_out, (("height", 1), ("width", 2)), 1)
    following = shifted(padded[:2], "tm", -1)
    extended = jnp.concatenate([padded, following], axis=0)
    act_cot = jnp.zeros((flat_act.shape[0], channels), jnp.float32)
    blocks = []
    for lag_t in range(3):
        for lag_h in range(3):
            for lag_w in range(3):
                window = extended[
                    2 - lag_t : 2 - lag_t + frame_count,
                    2 - lag_h : 2 - lag_h + row_count,
                    2 - lag_w : 2 - lag_w + col_count,
                ].reshape(-1, channels)
                act_cot = act_cot + lax.dot_general(
                    window,
                    weight[lag_t, lag_h, lag_w],
                    (((1,), (1,)), ((), ())),
                    preferred_element_type=jnp.float32,
                )
                blocks.append(
                    lax.dot_general(
                        flat_act,
                        window,
                        (((0,), (0,)), ((), ())),
                        preferred_element_type=jnp.float32,
                    )
                )
    act_cot = act_cot.reshape(frame_count, row_count, col_count, channels)
    is_last = lax.axis_index("tm") == lax.axis_size("tm") - 1
    tail_cot = jnp.where(
        is_last, future_cot.astype(jnp.float32), jnp.zeros(future_cot.shape, jnp.float32)
    )
    act_cot = jnp.concatenate(
        [act_cot[: frame_count - 2], act_cot[frame_count - 2 :] + tail_cot], axis=0
    )
    scaled = act_cot * sigmoid_val * (1.0 + pre_act * (1.0 - sigmoid_val)) * gain
    scaled_groups = scaled.reshape(frame_count, row_count, col_count, groups, group_width)
    sum_first = jnp.sum(scaled_groups, axis=(1, 2, 4))
    sum_second = jnp.sum(scaled_groups * centred, axis=(1, 2, 4))
    total_first, total_second = lax.psum((sum_first, sum_second), ("height", "width"))
    count = row_count * lax.axis_size("height") * col_count * lax.axis_size("width") * group_width
    first = total_first / count
    second = total_second / count
    corrected = rstd_saved[:, None, None, :, None] * (
        scaled_groups - first[:, None, None, :, None] - centred * second[:, None, None, :, None]
    )
    input_cot = (
        grad_out.astype(jnp.float32)
        + corrected.reshape(frame_count, row_count, col_count, channels)
    ).astype(jnp.bfloat16)
    all_cells = (
        frame_count
        * lax.axis_size("tm")
        * row_count
        * lax.axis_size("height")
        * col_count
        * lax.axis_size("width")
    )
    grad_scale = 1.0 / math.sqrt(all_cells)
    local_weight = jnp.stack(blocks).reshape(27 * channels, channels) * grad_scale
    weight_grad = reduced_share(local_weight)
    return (input_cot, weight_grad)


def solution(mesh):
    placed = (
        P("tm", "height", "width", None),
        P("tm", "height", "width", None),
        P("tm", None),
        P("tm", None),
        P(),
        P(),
        P(),
        P(None, "height", "width", None),
    )
    return jax.shard_map(
        on_device,
        mesh=mesh,
        in_specs=placed,
        out_specs=(P("tm", "height", "width", None), P("tm", None)),
        check_vma=False,
    )
```

```python
import functools
import math

import jax
import jax.numpy as jnp
from jax import lax
from jax.experimental import pallas as pl
from jax.experimental.pallas import tpu as pltpu
from jax.sharding import PartitionSpec as P

LEAD = 8
VMEM_BYTES = 56 * 1024 * 1024


def exchanged(value, axis, distance):
    count = lax.axis_size(axis)
    return lax.ppermute(value, axis, [(i, i ^ distance) for i in range(count)])


def shifted(value, axis, steps):
    count = lax.axis_size(axis)
    initial, last = (max(0, -steps), min(count, count - steps))
    return lax.ppermute(value, axis, [(source, source + steps) for source in range(initial, last)])


def power_of_two(count):
    return count & (count - 1) == 0


def paired():
    return lax.axis_size("height") == 2 and lax.axis_size("width") == 2


def kept_rows(rows):
    return -(-rows // 16) * 8


def joined(low, high, rows):
    kept = low.shape[0]
    return jnp.concatenate([low, high[2 * kept - rows :]], axis=0)


def in_halves(blocks, rows):
    return paired() and power_of_two(blocks) and rows % 16 == 0


def reduced_share(mine, theirs, rows):
    blocks = mine.shape[0]
    value = mine + exchanged(theirs, "width", 1)
    half = value.shape[1]
    kept = kept_rows(half)
    row_side = lax.axis_index("height")
    col_side = lax.axis_index("width")
    near = lax.dynamic_slice_in_dim(value, row_side * (half - kept), kept, 1)
    far = lax.dynamic_slice_in_dim(value, (1 - row_side) * (half - kept), kept, 1)
    value = near + exchanged(far.astype(jnp.bfloat16), "height", 1).astype(jnp.float32)
    place = lax.axis_index("tm")
    distance = 1
    while distance < blocks:
        side = (place // distance) % 2
        split = value.reshape(value.shape[0] // 2, 2, *value.shape[1:])
        near = lax.dynamic_index_in_dim(split, side, 1, keepdims=False)
        far = lax.dynamic_index_in_dim(split, 1 - side, 1, keepdims=False)
        wire = jnp.float32 if split.shape[0] == 1 else jnp.bfloat16
        value = near + exchanged(far.astype(wire), "tm", distance).astype(jnp.float32)
        distance *= 2
    own = value[0]
    beside = exchanged(own, "width", 1)
    below = exchanged(own, "height", 1)
    across = lax.ppermute(own, ("height", "width"), [(i, 3 - i) for i in range(4)])
    mine_half = joined(
        jnp.where(row_side == 0, own, below), jnp.where(row_side == 0, below, own), half
    )
    other_half = joined(
        jnp.where(row_side == 0, beside, across), jnp.where(row_side == 0, across, beside), half
    )
    return joined(
        jnp.where(col_side == 0, mine_half, other_half),
        jnp.where(col_side == 0, other_half, mine_half),
        rows,
    )


def group_matrix(rows, cols, row_width, col_width):
    row = lax.broadcasted_iota(jnp.int32, (rows, cols), 0) // row_width
    col = lax.broadcasted_iota(jnp.int32, (rows, cols), 1) // col_width
    return (row == col).astype(jnp.float32)


def exact_dot(left, right):
    return lax.dot_general(
        left,
        right,
        (((1,), (0,)), ((), ())),
        precision=lax.Precision.HIGHEST,
        preferred_element_type=jnp.float32,
    )


def per_channel(value, channels):
    groups = value.shape[1]
    return exact_dot(value, group_matrix(groups, channels, 1, channels // groups))


def act_kernel(features_ref, mean_ref, rstd_ref, gain_ref, bias_ref, act_ref):
    frames, rows, cols, channels = features_ref.shape
    cells = rows * cols
    mean = per_channel(mean_ref[...], channels)
    rstd = per_channel(rstd_ref[...], channels)
    for t in range(frames):
        value = features_ref[t].astype(jnp.float32).reshape(cells, channels)
        centred = (value - mean[t : t + 1]) * rstd[t : t + 1]
        pre_act = centred * gain_ref[...] + bias_ref[...]
        act = (pre_act * jax.nn.sigmoid(pre_act)).astype(jnp.bfloat16)
        act_ref[:, t * cells : (t + 1) * cells] = act.T


def fill_pair(grad_ref, halo_ref, row_ref, col_ref, corner_ref, tail_ref, stage_ref):
    frames, rows, cols, channels = grad_ref.shape
    extra = halo_ref.shape[0]
    row_side = lax.axis_index("height")
    col_side = lax.axis_index("width")
    rim_row = (1 - row_side) * (rows + 1)
    total = frames + extra
    for f in range(total):
        zeros = jnp.zeros((rows + 2, LEAD, channels), jnp.float32)
        stage_ref[f, :, 0:LEAD, :] = zeros
        stage_ref[f, :, LEAD + cols :, :] = zeros
        empty = jnp.zeros((cols, channels), jnp.float32)
        stage_ref[f, 0, LEAD : LEAD + cols, :] = empty
        stage_ref[f, rows + 1, LEAD : LEAD + cols, :] = empty
        inner = grad_ref[f] if f < frames else halo_ref[f - frames]
        stage_ref[f, 1 : rows + 1, LEAD : LEAD + cols, :] = inner.astype(jnp.float32)
        rim = row_ref[f] if f < frames else tail_ref[f - frames, 0:cols]
        stage_ref[f, rim_row, LEAD : LEAD + cols, :] = rim.astype(jnp.float32)

    def fill_columns(at):
        for f in range(total):
            if f < frames:
                column, corner = col_ref[f], corner_ref[f : f + 1]
            else:
                column = tail_ref[f - frames, cols : cols + rows]
                corner = tail_ref[f - frames, cols + rows : cols + rows + 1]
            column = column.astype(jnp.float32)
            for r in range(rows):
                stage_ref[f, r + 1, at : at + 1, :] = column[r : r + 1]
            stage_ref[f, rim_row, at : at + 1, :] = corner.astype(jnp.float32)

    @pl.when(col_side == 1)
    def _():
        fill_columns(LEAD - 1)

    @pl.when(col_side == 0)
    def _():
        fill_columns(LEAD + cols)


def weight_kernel(rows_out, scale, pair, halves, *refs):
    if pair:
        act_ref, grad_ref, halo_ref, row_ref, col_ref, corner_ref, tail_ref = refs[:7]
        refs = refs[7:]
    else:
        act_ref, stage_in_ref = refs[:2]
        refs = refs[2:]
    window_ref, outs, (stage_ref, sum_ref) = refs[0], refs[1:-2], refs[-2:]
    total, rows_ext, cols, wide = window_ref.shape
    rows = rows_ext - 2
    channels = wide // 3
    cells = rows * cols
    frames = act_ref.shape[1] // cells
    if pair:
        fill_pair(grad_ref, halo_ref, row_ref, col_ref, corner_ref, tail_ref, stage_ref)
    else:
        stage_ref[...] = stage_in_ref[...].astype(jnp.float32)

    def widen(f, carry):
        for e in range(3):
            at = LEAD - 1 + e
            window_ref[f, :, :, e * channels : (e + 1) * channels] = stage_ref[
                f, :, at : at + cols, :
            ].astype(jnp.bfloat16)
        return carry

    lax.fori_loop(0, total, widen, 0)

    for lag_t in range(3):
        for lag_h in range(3):
            acc = None
            for t in range(frames):
                window = window_ref[t + 2 - lag_t, 2 - lag_h : 2 - lag_h + rows]
                term = lax.dot_general(
                    act_ref[:, t * cells : (t + 1) * cells],
                    window.reshape(cells, wide),
                    (((1,), (0,)), ((), ())),
                    preferred_element_type=jnp.float32,
                )
                acc = term if acc is None else acc + term
            acc = acc * scale
            for lag_w in range(3):
                e = 2 - lag_w
                at = ((lag_t * 3 + lag_h) * 3 + lag_w) * channels
                sum_ref[at : at + channels, :] = acc[:, e * channels : (e + 1) * channels]
    if not halves:
        outs[0][...] = sum_ref[...]
        return
    mine_ref, theirs_ref = outs
    col_side = lax.axis_index("width")
    half = rows_out // 2

    def place(low_ref, high_ref):
        for block in range(mine_ref.shape[0]):
            at = block * rows_out
            low_ref[block] = sum_ref[at : at + half, :]
            high_ref[block] = sum_ref[at + half : at + rows_out, :]

    @pl.when(col_side == 0)
    def _():
        place(mine_ref, theirs_ref)

    @pl.when(col_side == 1)
    def _():
        place(theirs_ref, mine_ref)


def conv_kernel(
    window_ref,
    weight_ref,
    future_ref,
    features_ref,
    mean_ref,
    rstd_ref,
    gain_ref,
    bias_ref,
    scaled_ref,
    sums_ref,
):
    frames, rows, cols, channels = features_ref.shape
    cells = rows * cols
    wide = 3 * channels
    mean = per_channel(mean_ref[...], channels)
    rstd = per_channel(rstd_ref[...], channels)
    is_last = lax.axis_index("tm") == lax.axis_size("tm") - 1
    for t in range(frames):
        acc = None
        for lag_t in range(3):
            for lag_h in range(3):
                window = window_ref[t + 2 - lag_t, 2 - lag_h : 2 - lag_h + rows]
                taps = jnp.concatenate(
                    [weight_ref[lag_t, lag_h, 2 - e] for e in range(3)], axis=1
                )
                term = lax.dot_general(
                    window.reshape(cells, wide),
                    taps,
                    (((1,), (1,)), ((), ())),
                    preferred_element_type=jnp.float32,
                )
                acc = term if acc is None else acc + term
        later = t - (frames - future_ref.shape[0])
        if later >= 0:
            tail = future_ref[later].astype(jnp.float32).reshape(cells, channels)
            acc = acc + jnp.where(is_last, tail, jnp.zeros_like(tail))
        value = features_ref[t].astype(jnp.float32).reshape(cells, channels)
        centred = (value - mean[t : t + 1]) * rstd[t : t + 1]
        pre_act = centred * gain_ref[...] + bias_ref[...]
        sig = jax.nn.sigmoid(pre_act)
        scaled = acc * sig * (1.0 + pre_act * (1.0 - sig)) * gain_ref[...]
        scaled_ref[t] = scaled.reshape(rows, cols, channels)
        sums_ref[t : t + 1, :] = jnp.sum(scaled, axis=0, keepdims=True)
        sums_ref[frames + t : frames + t + 1, :] = jnp.sum(
            scaled * centred, axis=0, keepdims=True
        )


def final_kernel(count, terms, *refs):
    parts, (scaled_ref, features_ref, grad_ref, mean_ref, rstd_ref, out_ref) = (
        refs[:terms],
        refs[terms:],
    )
    frames, rows, cols, channels = features_ref.shape
    groups = mean_ref.shape[1]
    mean = per_channel(mean_ref[...], channels)
    rstd = per_channel(rstd_ref[...], channels)
    total = parts[0][...]
    for part in parts[1:]:
        total = total + part[...]
    width = channels // groups
    means = exact_dot(total, group_matrix(channels, channels, width, width)) / count
    for t in range(frames):
        value = features_ref[t].astype(jnp.float32)
        centred = (value - mean[t : t + 1]) * rstd[t : t + 1]
        first = means[t : t + 1]
        second = means[frames + t : frames + t + 1]
        corrected = rstd[t : t + 1] * (scaled_ref[t] - first - centred * second)
        out_ref[t] = (grad_ref[t].astype(jnp.float32) + corrected).astype(jnp.bfloat16)


def call(kernel, out_shape, scratch=(), flops=0, moved=0):
    return pl.pallas_call(
        kernel,
        out_shape=out_shape,
        scratch_shapes=list(scratch),
        compiler_params=pltpu.CompilerParams(vmem_limit_bytes=VMEM_BYTES),
        cost_estimate=pl.CostEstimate(flops=flops, bytes_accessed=moved, transcendentals=0),
    )


def extended(cells, sides, width):
    for axis, dim in sides:
        head = lax.slice_in_dim(cells, 0, width, axis=dim)
        tail = lax.slice_in_dim(cells, cells.shape[dim] - width, cells.shape[dim], axis=dim)
        cells = jnp.concatenate(
            [shifted(tail, axis, 1), cells, shifted(head, axis, -1)], axis=dim
        )
    return cells


def rims(grad_out, extra):
    frames, rows, cols, channels = grad_out.shape
    row_side = lax.axis_index("height")
    col_side = lax.axis_index("width")
    row_at = (1 - row_side) * (rows - 1)
    col_at = (1 - col_side) * (cols - 1)
    row = lax.dynamic_slice_in_dim(grad_out, row_at, 1, 1)[:, 0]
    col = lax.dynamic_slice_in_dim(grad_out, col_at, 1, 2)[:, :, 0]
    corner = lax.dynamic_slice_in_dim(row, col_at, 1, 1)[:, 0]
    halo = shifted(grad_out[:extra], "tm", -1)
    row = exchanged(row, "height", 1)
    col = exchanged(col, "width", 1)
    corner = lax.ppermute(corner, ("height", "width"), [(i, 3 - i) for i in range(4)])
    packed = jnp.concatenate([row[:extra], col[:extra], corner[:extra, None]], axis=1)
    return halo, row, col, corner, shifted(packed, "tm", -1)


def on_device(features, grad_out, mean_saved, rstd_saved, gain, bias, weight, future_cot):
    frames, rows, cols, channels = features.shape
    extra = weight.shape[0] - 1
    cells = rows * cols
    groups = mean_saved.shape[1]
    blocks = lax.axis_size("tm")
    taps = math.prod(weight.shape[:3])
    rows_out = taps * channels // blocks
    positions = cells * lax.axis_size("height") * lax.axis_size("width")
    grad_scale = 1.0 / math.sqrt(positions * frames * blocks)
    gain = gain.reshape(1, channels)
    bias = bias.reshape(1, channels)
    pair = paired()
    halves = in_halves(blocks, rows_out)
    f32 = jnp.float32

    if pair:
        sources = (grad_out, *rims(grad_out, extra))
    else:
        padded = extended(grad_out, (("height", 1), ("width", 2)), 1)
        whole = jnp.concatenate([padded, shifted(padded[:extra], "tm", -1)], axis=0)
        sources = (jnp.pad(whole, ((0, 0), (0, 0), (LEAD - 1, LEAD - 1), (0, 0))),)

    act = call(
        act_kernel,
        jax.ShapeDtypeStruct((channels, frames * cells), jnp.bfloat16),
        flops=20 * frames * cells * channels,
        moved=4 * frames * cells * channels,
    )(features, mean_saved, rstd_saved, gain, bias)

    total = frames + extra
    window_shape = (total, rows + 2, cols, 3 * channels)
    work = 2 * taps * channels * channels * frames * cells
    if halves:
        half_shape = jax.ShapeDtypeStruct((blocks, rows_out // 2, channels), f32)
        sum_shapes = (half_shape, half_shape)
    else:
        sum_shapes = (jax.ShapeDtypeStruct((taps * channels, channels), f32),)
    window, *sums = call(
        functools.partial(weight_kernel, rows_out, grad_scale, pair, halves),
        (jax.ShapeDtypeStruct(window_shape, jnp.bfloat16), *sum_shapes),
        scratch=(
            pltpu.VMEM((total, rows + 2, cols + 2 * LEAD, channels), f32),
            pltpu.VMEM((taps * channels, channels), f32),
        ),
        flops=work,
        moved=8 * 1024 * 1024,
    )(act, *sources)

    if halves:
        weight_grad = reduced_share(*sums, rows_out)
    else:
        share = lax.psum_scatter(sums[0], "tm", scatter_dimension=0, tiled=True)
        weight_grad = lax.psum(share, ("height", "width"))

    scaled, local = call(
        conv_kernel,
        (
            jax.ShapeDtypeStruct((frames, rows, cols, channels), f32),
            jax.ShapeDtypeStruct((2 * frames, channels), f32),
        ),
        flops=work,
        moved=8 * 1024 * 1024,
    )(window, weight, future_cot, features, mean_saved, rstd_saved, gain, bias)

    if pair:
        parts = [
            local,
            exchanged(local, "width", 1),
            exchanged(local, "height", 1),
            lax.ppermute(local, ("height", "width"), [(i, 3 - i) for i in range(4)]),
        ]
    else:
        parts = [lax.psum(local, ("height", "width"))]
    input_cot = call(
        functools.partial(final_kernel, positions * (channels // groups), len(parts)),
        jax.ShapeDtypeStruct(features.shape, jnp.bfloat16),
        flops=20 * frames * cells * channels,
        moved=10 * frames * cells * channels,
    )(*parts, scaled, features, grad_out, mean_saved, rstd_saved)
    return (input_cot, weight_grad)


def solution(mesh):
    placed = (
        P("tm", "height", "width", None),
        P("tm", "height", "width", None),
        P("tm", None),
        P("tm", None),
        P(),
        P(),
        P(),
        P(None, "height", "width", None),
    )
    return jax.shard_map(
        on_device,
        mesh=mesh,
        in_specs=placed,
        out_specs=(P("tm", "height", "width", None), P("tm", None)),
        check_vma=False,
    )
```

```python
import functools
import math

import jax
import jax.numpy as jnp
from jax import lax
from jax.experimental import pallas as pl
from jax.experimental.pallas import tpu as pltpu
from jax.sharding import PartitionSpec as P


LEAD = 8
VMEM_BYTES = 12 * 1024 * 1024


def exchanged(value, axis, distance):
    count = lax.axis_size(axis)
    return lax.ppermute(value, axis, [(i, i ^ distance) for i in range(count)])


def shifted(value, axis, steps):
    count = lax.axis_size(axis)
    initial, last = (max(0, -steps), min(count, count - steps))
    return lax.ppermute(value, axis, [(source, source + steps) for source in range(initial, last)])


def power_of_two(count):
    return count & (count - 1) == 0


def paired():
    return lax.axis_size("height") == 2 and lax.axis_size("width") == 2


def kept_rows(rows):
    return -(-rows // 16) * 8


def joined(low, high, rows):
    kept = low.shape[0]
    return jnp.concatenate([low, high[2 * kept - rows :]], axis=0)


def in_halves(blocks, rows):
    return paired() and power_of_two(blocks) and rows % 16 == 0


def reduced_share(mine, theirs, rows):
    blocks = mine.shape[0]
    value = mine + exchanged(theirs, "width", 1)
    half = value.shape[1]
    kept = kept_rows(half)
    row_side = lax.axis_index("height")
    col_side = lax.axis_index("width")
    near = lax.dynamic_slice_in_dim(value, row_side * (half - kept), kept, 1)
    far = lax.dynamic_slice_in_dim(value, (1 - row_side) * (half - kept), kept, 1)
    value = near + exchanged(far.astype(jnp.bfloat16), "height", 1).astype(jnp.float32)
    place = lax.axis_index("tm")
    distance = 1
    while blocks // distance > 4:
        side = (place // distance) % 2
        split = value.reshape(value.shape[0] // 2, 2, *value.shape[1:])
        near = lax.dynamic_index_in_dim(split, side, 1, keepdims=False)
        far = lax.dynamic_index_in_dim(split, 1 - side, 1, keepdims=False)
        value = near + exchanged(far.astype(jnp.bfloat16), "tm", distance).astype(jnp.float32)
        distance *= 2
    left = blocks // distance
    spot = place // distance
    own = lax.dynamic_index_in_dim(value, spot, 0, keepdims=False)
    for step in range(1, left):
        far = lax.dynamic_index_in_dim(value, spot ^ step, 0, keepdims=False)
        own = own + exchanged(far.astype(jnp.bfloat16), "tm", step * distance).astype(jnp.float32)
    beside = exchanged(own, "width", 1)
    below = exchanged(own, "height", 1)
    across = lax.ppermute(own, ("height", "width"), [(i, 3 - i) for i in range(4)])
    mine_half = joined(
        jnp.where(row_side == 0, own, below), jnp.where(row_side == 0, below, own), half
    )
    other_half = joined(
        jnp.where(row_side == 0, beside, across), jnp.where(row_side == 0, across, beside), half
    )
    return joined(
        jnp.where(col_side == 0, mine_half, other_half),
        jnp.where(col_side == 0, other_half, mine_half),
        rows,
    )


def group_matrix(rows, cols, row_width, col_width):
    row = lax.broadcasted_iota(jnp.int32, (rows, cols), 0) // row_width
    col = lax.broadcasted_iota(jnp.int32, (rows, cols), 1) // col_width
    return (row == col).astype(jnp.float32)


def exact_dot(left, right):
    return lax.dot_general(
        left,
        right,
        (((1,), (0,)), ((), ())),
        precision=lax.Precision.HIGHEST,
        preferred_element_type=jnp.float32,
    )


def per_channel(value, channels):
    groups = value.shape[1]
    return exact_dot(value, group_matrix(groups, channels, 1, channels // groups))


def act_kernel(features_ref, mean_ref, rstd_ref, gain_ref, bias_ref, act_ref):
    frames, rows, cols, channels = features_ref.shape
    cells = rows * cols
    mean = per_channel(mean_ref[...], channels)
    rstd = per_channel(rstd_ref[...], channels)
    for t in range(frames):
        value = features_ref[t].astype(jnp.float32).reshape(cells, channels)
        centred = (value - mean[t : t + 1]) * rstd[t : t + 1]
        pre_act = centred * gain_ref[...] + bias_ref[...]
        act = (pre_act * jax.nn.sigmoid(pre_act)).astype(jnp.bfloat16)
        act_ref[:, t * cells : (t + 1) * cells] = act.T


def fill_pair(stage_ref, inner_ref, row_of, col_of, corner_of):
    total, rows, cols, channels = inner_ref.shape
    row_side = lax.axis_index("height")
    col_side = lax.axis_index("width")
    rim_row = (1 - row_side) * (rows + 1)
    for f in range(total):
        zeros = jnp.zeros((rows + 2, LEAD, channels), jnp.float32)
        stage_ref[f, :, 0:LEAD, :] = zeros
        stage_ref[f, :, LEAD + cols :, :] = zeros
        empty = jnp.zeros((cols, channels), jnp.float32)
        stage_ref[f, 0, LEAD : LEAD + cols, :] = empty
        stage_ref[f, rows + 1, LEAD : LEAD + cols, :] = empty
        stage_ref[f, 1 : rows + 1, LEAD : LEAD + cols, :] = inner_ref[f].astype(jnp.float32)
        stage_ref[f, rim_row, LEAD : LEAD + cols, :] = row_of(f).astype(jnp.float32)

    def fill_columns(at):
        for f in range(total):
            column = col_of(f).astype(jnp.float32)
            for r in range(rows):
                stage_ref[f, r + 1, at : at + 1, :] = column[r : r + 1]
            stage_ref[f, rim_row, at : at + 1, :] = corner_of(f).astype(jnp.float32)

    @pl.when(col_side == 1)
    def _():
        fill_columns(LEAD - 1)

    @pl.when(col_side == 0)
    def _():
        fill_columns(LEAD + cols)


def widen(stage_ref, window_ref):
    total, _, cols, wide = window_ref.shape
    channels = wide // 3

    def one(f, carry):
        for e in range(3):
            at = LEAD - 1 + e
            window_ref[f, :, :, e * channels : (e + 1) * channels] = stage_ref[
                f, :, at : at + cols, :
            ].astype(jnp.bfloat16)
        return carry

    lax.fori_loop(0, total, one, 0)


def tap_sums(act_ref, window_of, frames, rows, cols, lag_h):
    cells = rows * cols
    acc = None
    for t in range(frames):
        window = window_of(t)[lag_h : lag_h + rows]
        term = lax.dot_general(
            act_ref[:, t * cells : (t + 1) * cells],
            window.reshape(cells, window.shape[-1]),
            (((1,), (0,)), ((), ())),
            preferred_element_type=jnp.float32,
        )
        acc = term if acc is None else acc + term
    return acc


def near_kernel(scale, pair, act_ref, *refs):
    sources, (window_ref, sum_ref, stage_ref) = refs[:-3], refs[-3:]
    frames, rows_ext, cols, wide = window_ref.shape
    rows = rows_ext - 2
    channels = wide // 3
    if pair:
        grad_ref, row_ref, col_ref, corner_ref = sources
        fill_pair(
            stage_ref,
            grad_ref,
            lambda f: row_ref[f],
            lambda f: col_ref[f],
            lambda f: corner_ref[f : f + 1],
        )
    else:
        stage_ref[...] = sources[0][...].astype(jnp.float32)
    widen(stage_ref, window_ref)
    for lag_h in range(3):
        acc = scale * tap_sums(act_ref, lambda t: window_ref.at[t], frames, rows, cols, 2 - lag_h)
        for lag_w in range(3):
            e = 2 - lag_w
            at = (lag_h * 3 + lag_w) * channels
            sum_ref[at : at + channels, :] = acc[:, e * channels : (e + 1) * channels]


def far_kernel(rows_out, scale, pair, halves, act_ref, near_ref, near_sum_ref, *refs):
    count = 2 if pair else 1
    sources, window_ref, outs, (stage_ref, sum_ref) = (
        refs[:count],
        refs[count],
        refs[count + 1 : -2],
        refs[-2:],
    )
    extra, rows_ext, cols, wide = window_ref.shape
    frames = near_ref.shape[0]
    rows = rows_ext - 2
    channels = wide // 3
    if pair:
        halo_ref, tail_ref = sources
        fill_pair(
            stage_ref,
            halo_ref,
            lambda f: tail_ref[f, 0:cols],
            lambda f: tail_ref[f, cols : cols + rows],
            lambda f: tail_ref[f, cols + rows : cols + rows + 1],
        )
    else:
        stage_ref[...] = sources[0][...].astype(jnp.float32)
    widen(stage_ref, window_ref)

    def window_of(f):
        return near_ref.at[f] if f < frames else window_ref.at[f - frames]

    for lag_t in range(extra):
        for lag_h in range(3):
            acc = scale * tap_sums(
                act_ref, lambda t: window_of(t + extra - lag_t), frames, rows, cols, 2 - lag_h
            )
            for lag_w in range(3):
                e = 2 - lag_w
                at = ((lag_t * 3 + lag_h) * 3 + lag_w) * channels
                sum_ref[at : at + channels, :] = acc[:, e * channels : (e + 1) * channels]
    done = extra * 9 * channels
    sum_ref[done:, :] = near_sum_ref[...]
    if not halves:
        outs[0][...] = sum_ref[...]
        return
    mine_ref, theirs_ref = outs
    col_side = lax.axis_index("width")
    half = rows_out // 2

    def place(low_ref, high_ref):
        for block in range(mine_ref.shape[0]):
            at = block * rows_out
            low_ref[block] = sum_ref[at : at + half, :]
            high_ref[block] = sum_ref[at + half : at + rows_out, :]

    @pl.when(col_side == 0)
    def _():
        place(mine_ref, theirs_ref)

    @pl.when(col_side == 1)
    def _():
        place(theirs_ref, mine_ref)


def conv_kernel(
    near_ref,
    far_ref,
    weight_ref,
    future_ref,
    features_ref,
    mean_ref,
    rstd_ref,
    gain_ref,
    bias_ref,
    scaled_ref,
    sums_ref,
):
    frames, rows, cols, channels = features_ref.shape
    cells = rows * cols
    wide = 3 * channels
    mean = per_channel(mean_ref[...], channels)
    rstd = per_channel(rstd_ref[...], channels)
    is_last = lax.axis_index("tm") == lax.axis_size("tm") - 1
    for t in range(frames):
        acc = None
        for lag_t in range(3):
            for lag_h in range(3):
                f = t + far_ref.shape[0] - lag_t
                source = near_ref.at[f] if f < frames else far_ref.at[f - frames]
                window = source[2 - lag_h : 2 - lag_h + rows]
                taps = jnp.concatenate(
                    [weight_ref[lag_t, lag_h, 2 - e] for e in range(3)], axis=1
                )
                term = lax.dot_general(
                    window.reshape(cells, wide),
                    taps,
                    (((1,), (1,)), ((), ())),
                    preferred_element_type=jnp.float32,
                )
                acc = term if acc is None else acc + term
        later = t - (frames - future_ref.shape[0])
        if later >= 0:
            tail = future_ref[later].astype(jnp.float32).reshape(cells, channels)
            acc = acc + jnp.where(is_last, tail, jnp.zeros_like(tail))
        value = features_ref[t].astype(jnp.float32).reshape(cells, channels)
        centred = (value - mean[t : t + 1]) * rstd[t : t + 1]
        pre_act = centred * gain_ref[...] + bias_ref[...]
        sig = jax.nn.sigmoid(pre_act)
        scaled = acc * sig * (1.0 + pre_act * (1.0 - sig)) * gain_ref[...]
        scaled_ref[t] = scaled.reshape(rows, cols, channels)
        sums_ref[t : t + 1, :] = jnp.sum(scaled, axis=0, keepdims=True)
        sums_ref[frames + t : frames + t + 1, :] = jnp.sum(
            scaled * centred, axis=0, keepdims=True
        )


def final_kernel(count, terms, *refs):
    parts, (scaled_ref, features_ref, grad_ref, mean_ref, rstd_ref, out_ref) = (
        refs[:terms],
        refs[terms:],
    )
    frames, _, _, channels = features_ref.shape
    groups = mean_ref.shape[1]
    mean = per_channel(mean_ref[...], channels)
    rstd = per_channel(rstd_ref[...], channels)
    total = parts[0][...]
    for part in parts[1:]:
        total = total + part[...]
    width = channels // groups
    means = exact_dot(total, group_matrix(channels, channels, width, width)) / count
    for t in range(frames):
        value = features_ref[t].astype(jnp.float32)
        centred = (value - mean[t : t + 1]) * rstd[t : t + 1]
        first = means[t : t + 1]
        second = means[frames + t : frames + t + 1]
        corrected = rstd[t : t + 1] * (scaled_ref[t] - first - centred * second)
        out_ref[t] = (grad_ref[t].astype(jnp.float32) + corrected).astype(jnp.bfloat16)


def call(kernel, out_shape, scratch=(), flops=0, moved=0, out_specs=None):
    here = pl.BlockSpec(memory_space=pltpu.VMEM)

    def run(*args):
        return pl.pallas_call(
            kernel,
            out_shape=out_shape,
            in_specs=[here] * len(args),
            out_specs=out_specs or jax.tree.map(lambda _: here, out_shape),
            scratch_shapes=list(scratch),
            compiler_params=pltpu.CompilerParams(vmem_limit_bytes=VMEM_BYTES),
            cost_estimate=pl.CostEstimate(flops=flops, bytes_accessed=moved, transcendentals=0),
        )(*args)

    return run


def extended(cells, sides, width):
    for axis, dim in sides:
        head = lax.slice_in_dim(cells, 0, width, axis=dim)
        tail = lax.slice_in_dim(cells, cells.shape[dim] - width, cells.shape[dim], axis=dim)
        cells = jnp.concatenate(
            [shifted(tail, axis, 1), cells, shifted(head, axis, -1)], axis=dim
        )
    return cells


def rims(grad_out, extra):
    _, rows, cols, _ = grad_out.shape
    row_side = lax.axis_index("height")
    col_side = lax.axis_index("width")
    row_at = (1 - row_side) * (rows - 1)
    col_at = (1 - col_side) * (cols - 1)
    halo = shifted(grad_out[:extra], "tm", -1)
    row = lax.dynamic_slice_in_dim(grad_out, row_at, 1, 1)[:, 0]
    col = lax.dynamic_slice_in_dim(grad_out, col_at, 1, 2)[:, :, 0]
    corner = lax.dynamic_slice_in_dim(row, col_at, 1, 1)[:, 0]
    row = exchanged(row, "height", 1)
    col = exchanged(col, "width", 1)
    corner = lax.ppermute(corner, ("height", "width"), [(i, 3 - i) for i in range(4)])
    packed = jnp.concatenate([row[:extra], col[:extra], corner[:extra, None]], axis=1)
    tail = shifted(packed, "tm", -1)
    return (grad_out, row, col, corner), (halo, tail)


def on_device(features, grad_out, mean_saved, rstd_saved, gain, bias, weight, future_cot):
    frames, rows, cols, channels = features.shape
    extra = weight.shape[0] - 1
    cells = rows * cols
    groups = mean_saved.shape[1]
    blocks = lax.axis_size("tm")
    taps = math.prod(weight.shape[:3])
    rows_out = taps * channels // blocks
    positions = cells * lax.axis_size("height") * lax.axis_size("width")
    grad_scale = 1.0 / math.sqrt(positions * frames * blocks)
    gain = gain.reshape(1, channels)
    bias = bias.reshape(1, channels)
    pair = paired()
    halves = in_halves(blocks, rows_out)
    f32 = jnp.float32

    if pair:
        near_sources, far_sources = rims(grad_out, extra)
    else:
        padded = extended(grad_out, (("height", 1), ("width", 2)), 1)
        sides = ((0, 0), (0, 0), (LEAD - 1, LEAD - 1), (0, 0))
        near_sources = (jnp.pad(padded, sides),)
        far_sources = (jnp.pad(shifted(padded[:extra], "tm", -1), sides),)

    act = call(
        act_kernel,
        jax.ShapeDtypeStruct((channels, frames * cells), jnp.bfloat16),
        flops=20 * frames * cells * channels,
        moved=4 * frames * cells * channels,
    )(features, mean_saved, rstd_saved, gain, bias)

    def window_shape(count):
        return jax.ShapeDtypeStruct((count, rows + 2, cols, 3 * channels), jnp.bfloat16)

    def stage_shape(count):
        return pltpu.VMEM((count, rows + 2, cols + 2 * LEAD, channels), f32)

    work = 2 * taps * channels * channels * frames * cells
    part = taps // (extra + 1)
    near_window, near_sum = call(
        functools.partial(near_kernel, grad_scale, pair),
        (window_shape(frames), jax.ShapeDtypeStruct((part * channels, channels), f32)),
        scratch=(stage_shape(frames),),
        flops=work // 3,
        moved=4 * 1024 * 1024,
    )(act, *near_sources)

    if halves:
        half_shape = jax.ShapeDtypeStruct((blocks, rows_out // 2, channels), f32)
        sum_shapes = (half_shape, half_shape)
    else:
        sum_shapes = (jax.ShapeDtypeStruct((taps * channels, channels), f32),)
    far_window, *sums = call(
        functools.partial(far_kernel, rows_out, grad_scale, pair, halves),
        (window_shape(extra), *sum_shapes),
        scratch=(stage_shape(extra), pltpu.VMEM((taps * channels, channels), f32)),
        flops=2 * work // 3,
        moved=4 * 1024 * 1024,
    )(act, near_window, near_sum, *far_sources)

    if halves:
        weight_grad = reduced_share(*sums, rows_out)
    else:
        share = lax.psum_scatter(sums[0], "tm", scatter_dimension=0, tiled=True)
        weight_grad = lax.psum(share, ("height", "width"))

    scaled, local = call(
        conv_kernel,
        (
            jax.ShapeDtypeStruct((frames, rows, cols, channels), f32),
            jax.ShapeDtypeStruct((2 * frames, channels), f32),
        ),
        flops=work,
        moved=8 * 1024 * 1024,
    )(near_window, far_window, weight, future_cot, features, mean_saved, rstd_saved, gain, bias)

    if pair:
        parts = [local]
        parts.append(exchanged(local, "width", 1))
        parts.append(exchanged(local, "height", 1))
        parts.append(
            lax.ppermute(local, ("height", "width"), [(i, 3 - i) for i in range(4)])
        )
    else:
        parts = [lax.psum(local, ("height", "width"))]
    input_cot = call(
        functools.partial(final_kernel, positions * (channels // groups), len(parts)),
        jax.ShapeDtypeStruct(features.shape, jnp.bfloat16),
        flops=20 * frames * cells * channels,
        moved=10 * frames * cells * channels,
        out_specs=pl.BlockSpec(features.shape, lambda: (0, 0, 0, 0)),
    )(*parts, scaled, features, grad_out, mean_saved, rstd_saved)
    return (input_cot, weight_grad)


def solution(mesh):
    placed = (
        P("tm", "height", "width", None),
        P("tm", "height", "width", None),
        P("tm", None),
        P("tm", None),
        P(),
        P(),
        P(),
        P(None, "height", "width", None),
    )
    return jax.shard_map(
        on_device,
        mesh=mesh,
        in_specs=placed,
        out_specs=(P("tm", "height", "width", None), P("tm", None)),
        check_vma=False,
    )
```

```python
import functools
import math

import jax
import jax.numpy as jnp
from jax import lax
from jax.experimental import pallas as pl
from jax.experimental.pallas import tpu as pltpu
from jax.sharding import PartitionSpec as P


LEAD = 8
VMEM_BYTES = 12 * 1024 * 1024


def exchanged(value, axis, distance):
    count = lax.axis_size(axis)
    return lax.ppermute(value, axis, [(i, i ^ distance) for i in range(count)])


def shifted(value, axis, steps):
    count = lax.axis_size(axis)
    initial, last = (max(0, -steps), min(count, count - steps))
    return lax.ppermute(value, axis, [(source, source + steps) for source in range(initial, last)])


def power_of_two(count):
    return count & (count - 1) == 0


def paired():
    return lax.axis_size("height") == 2 and lax.axis_size("width") == 2


def kept_rows(rows):
    return -(-rows // 16) * 8


def in_halves(blocks, rows):
    return paired() and power_of_two(blocks) and blocks > 1 and rows % 16 == 0


def split_rows_kernel(mine_ref, got_ref, near_ref, far_ref):
    half, kept = mine_ref.shape[1], near_ref.shape[1]
    side = lax.axis_index("height")

    def place(low_ref, high_ref):
        for block in range(mine_ref.shape[0]):
            value = mine_ref[block] + got_ref[block]
            low_ref[block] = value[:kept].astype(low_ref.dtype)
            high_ref[block] = value[half - kept :].astype(high_ref.dtype)

    @pl.when(side == 0)
    def _():
        place(near_ref, far_ref)

    @pl.when(side == 1)
    def _():
        place(far_ref, near_ref)


def split_blocks_kernel(distance, mine_ref, got_ref, near_ref, far_ref):
    side = (lax.axis_index("tm") // distance) % 2
    for pair in range(near_ref.shape[0]):
        at = 2 * pair + side
        near_ref[pair] = mine_ref[at] + got_ref[at].astype(jnp.float32)
        at = 2 * pair + 1 - side
        far_ref[pair] = (mine_ref[at] + got_ref[at].astype(jnp.float32)).astype(far_ref.dtype)


def split_all_kernel(distance, mine_ref, got_ref, own_ref, *far_refs):
    spot = lax.axis_index("tm") // distance
    own_ref[...] = mine_ref[spot] + got_ref[spot].astype(jnp.float32)
    for step, far_ref in enumerate(far_refs, 1):
        at = lax.bitwise_xor(spot, step)
        far_ref[...] = (mine_ref[at] + got_ref[at].astype(jnp.float32)).astype(far_ref.dtype)


def add_kernel(own_ref, *refs):
    total = own_ref[...]
    for ref in refs[:-1]:
        total = total + ref[...].astype(jnp.float32)
    refs[-1][...] = total


def assemble_kernel(own_ref, beside_ref, below_ref, across_ref, out_ref):
    kept = own_ref.shape[0]
    half = out_ref.shape[0] // 2
    col_side = lax.axis_index("width")
    mine = pl.multiple_of(col_side * half, 8)
    other = pl.multiple_of((1 - col_side) * half, 8)

    def place(lows, highs):
        for at, low_ref, high_ref in zip((mine, other), lows, highs):
            out_ref[pl.ds(at, kept), :] = low_ref[...]
            out_ref[pl.ds(at + kept, half - kept), :] = high_ref[2 * kept - half :, :]

    @pl.when(lax.axis_index("height") == 0)
    def _():
        place((own_ref, beside_ref), (below_ref, across_ref))

    @pl.when(lax.axis_index("height") == 1)
    def _():
        place((below_ref, across_ref), (own_ref, beside_ref))


def reduced_share(mine, theirs, rows):
    blocks, half, channels = mine.shape
    kept = kept_rows(half)
    f32, wire = jnp.float32, jnp.bfloat16

    def pieces(count, dtype):
        return jax.ShapeDtypeStruct((count, kept, channels), dtype)

    def single(dtype):
        return jax.ShapeDtypeStruct((kept, channels), dtype)

    got = exchanged(theirs, "width", 1)
    near, far = call(split_rows_kernel, (pieces(blocks, f32), pieces(blocks, wire)))(mine, got)
    got = exchanged(far, "height", 1)
    distance = 1
    while blocks // distance > 4:
        count = near.shape[0] // 2
        near, far = call(
            functools.partial(split_blocks_kernel, distance),
            (pieces(count, f32), pieces(count, wire)),
        )(near, got)
        got = exchanged(far, "tm", distance)
        distance *= 2
    left = blocks // distance
    own, *fars = call(
        functools.partial(split_all_kernel, distance),
        (single(f32), *[single(wire)] * (left - 1)),
    )(near, got)
    arrived = []
    for step, far in enumerate(fars, 1):
        arrived.append(exchanged(far, "tm", step * distance))
    own = call(add_kernel, single(f32))(own, *arrived)
    below = exchanged(own, "height", 1)
    across = lax.ppermute(own, ("height", "width"), [(i, 3 - i) for i in range(4)])
    beside = exchanged(own, "width", 1)
    return call(
        assemble_kernel,
        jax.ShapeDtypeStruct((rows, channels), f32),
        out_specs=pl.BlockSpec((rows, channels), lambda: (0, 0)),
    )(own, beside, below, across)


def group_matrix(rows, cols, row_width, col_width):
    row = lax.broadcasted_iota(jnp.int32, (rows, cols), 0) // row_width
    col = lax.broadcasted_iota(jnp.int32, (rows, cols), 1) // col_width
    return (row == col).astype(jnp.float32)


def exact_dot(left, right):
    return lax.dot_general(
        left,
        right,
        (((1,), (0,)), ((), ())),
        precision=lax.Precision.HIGHEST,
        preferred_element_type=jnp.float32,
    )


def per_channel(value, channels):
    groups = value.shape[1]
    return exact_dot(value, group_matrix(groups, channels, 1, channels // groups))


def cut_kernel(grad_ref, halo_ref, row_ref, col_ref, corner_ref):
    frames, rows, cols, _ = grad_ref.shape
    halo_ref[...] = grad_ref[: halo_ref.shape[0]]
    row_at = (1 - lax.axis_index("height")) * (rows - 1)

    def columns(at):
        corners = []
        for f in range(frames):
            col_ref[f] = grad_ref[f].astype(jnp.float32)[:, at].astype(jnp.bfloat16)
            corners.append(grad_ref[f, row_at].astype(jnp.float32)[at : at + 1])
        corner_ref[...] = jnp.concatenate(corners, axis=0).astype(jnp.bfloat16)

    for f in range(frames):
        row_ref[f] = grad_ref[f, row_at]

    @pl.when(lax.axis_index("width") == 0)
    def _():
        columns(cols - 1)

    @pl.when(lax.axis_index("width") == 1)
    def _():
        columns(0)


def pack_kernel(row_ref, col_ref, corner_ref, tail_ref):
    cols, rows = row_ref.shape[1], col_ref.shape[1]
    for f in range(tail_ref.shape[0]):
        tail_ref[f, 0:cols] = row_ref[f]
        tail_ref[f, cols : cols + rows] = col_ref[f]
        tail_ref[f, cols + rows :] = corner_ref[f : f + 1]


def act_kernel(features_hbm, mean_hbm, rstd_hbm, gain_hbm, bias_hbm, act_ref, params_ref, *scratch):
    buffers, sems = scratch[:5], scratch[5]
    sources = (features_hbm, mean_hbm, rstd_hbm, gain_hbm, bias_hbm)
    copies = [
        pltpu.make_async_copy(source, buffer, sems.at[i])
        for i, (source, buffer) in enumerate(zip(sources, buffers))
    ]
    for copy in copies:
        copy.start()
    for copy in copies:
        copy.wait()
    features_ref, mean_ref, rstd_ref, gain_ref, bias_ref = buffers
    frames, rows, cols, channels = features_ref.shape
    cells = rows * cols
    mean = per_channel(mean_ref[...], channels)
    rstd = per_channel(rstd_ref[...], channels)
    gain, bias = gain_ref[...], bias_ref[...]
    params_ref[...] = jnp.concatenate([mean, rstd, gain, bias], axis=0)
    for t in range(frames):
        value = features_ref[t].astype(jnp.float32).reshape(cells, channels)
        centred = (value - mean[t : t + 1]) * rstd[t : t + 1]
        pre_act = centred * gain + bias
        act = (pre_act * jax.nn.sigmoid(pre_act)).astype(jnp.bfloat16)
        act_ref[:, t * cells : (t + 1) * cells] = act.T


def fill_pair(stage_ref, inner_ref, row_of, col_of, corner_of):
    total, rows, cols, channels = inner_ref.shape
    row_side = lax.axis_index("height")
    col_side = lax.axis_index("width")
    rim_row = (1 - row_side) * (rows + 1)
    for f in range(total):
        zeros = jnp.zeros((rows + 2, LEAD, channels), jnp.float32)
        stage_ref[f, :, 0:LEAD, :] = zeros
        stage_ref[f, :, LEAD + cols :, :] = zeros
        empty = jnp.zeros((cols, channels), jnp.float32)
        stage_ref[f, 0, LEAD : LEAD + cols, :] = empty
        stage_ref[f, rows + 1, LEAD : LEAD + cols, :] = empty
        stage_ref[f, 1 : rows + 1, LEAD : LEAD + cols, :] = inner_ref[f].astype(jnp.float32)
        stage_ref[f, rim_row, LEAD : LEAD + cols, :] = row_of(f).astype(jnp.float32)

    def fill_columns(at):
        for f in range(total):
            column = col_of(f).astype(jnp.float32)
            for r in range(rows):
                stage_ref[f, r + 1, at : at + 1, :] = column[r : r + 1]
            stage_ref[f, rim_row, at : at + 1, :] = corner_of(f).astype(jnp.float32)

    @pl.when(col_side == 1)
    def _():
        fill_columns(LEAD - 1)

    @pl.when(col_side == 0)
    def _():
        fill_columns(LEAD + cols)


def widen(stage_ref, window_ref):
    total, _, cols, wide = window_ref.shape
    channels = wide // 3

    def one(f, carry):
        for e in range(3):
            at = LEAD - 1 + e
            window_ref[f, :, :, e * channels : (e + 1) * channels] = stage_ref[
                f, :, at : at + cols, :
            ].astype(jnp.bfloat16)
        return carry

    lax.fori_loop(0, total, one, 0)


def tap_sums(act_ref, scale, pairs, window_of, shape, lag_t, add):
    rows, cols, channels = shape
    cells = rows * cols
    for lag_h in range(3):
        acc = None
        for t, f in pairs:
            window = window_of(f)[2 - lag_h : 2 - lag_h + rows]
            term = lax.dot_general(
                act_ref[:, t * cells : (t + 1) * cells],
                window.reshape(cells, window.shape[-1]),
                (((1,), (0,)), ((), ())),
                preferred_element_type=jnp.float32,
            )
            acc = term if acc is None else acc + term
        for lag_w in range(3):
            e = 2 - lag_w
            at = ((lag_t * 3 + lag_h) * 3 + lag_w) * channels
            if acc is None:
                value = jnp.zeros((channels, channels), jnp.float32)
            else:
                value = scale * acc[:, e * channels : (e + 1) * channels]
            add(at, value)


def near_kernel(scale, pair, extra, act_ref, *refs):
    sources, (window_ref, sum_ref, stage_ref) = refs[:-3], refs[-3:]
    frames, rows_ext, cols, wide = window_ref.shape
    shape = (rows_ext - 2, cols, wide // 3)
    if pair:
        grad_ref, row_ref, col_ref, corner_ref = sources
        fill_pair(
            stage_ref,
            grad_ref,
            lambda f: row_ref[f],
            lambda f: col_ref[f],
            lambda f: corner_ref[f : f + 1],
        )
    else:
        stage_ref[...] = sources[0][...].astype(jnp.float32)
    widen(stage_ref, window_ref)

    def put(at, value):
        sum_ref[at : at + value.shape[0], :] = value

    for lag_t in range(extra + 1):
        ahead = extra - lag_t
        pairs = [(t, t + ahead) for t in range(frames) if t + ahead < frames]
        tap_sums(act_ref, scale, pairs, lambda f: window_ref.at[f], shape, lag_t, put)


def far_kernel(rows_out, scale, pair, halves, frames, act_ref, near_sum_ref, *refs):
    count = 2 if pair else 1
    sources, window_ref, outs, (stage_ref, sum_ref) = (
        refs[:count],
        refs[count],
        refs[count + 1 : -2],
        refs[-2:],
    )
    extra, rows_ext, cols, wide = window_ref.shape
    rows = rows_ext - 2
    channels = wide // 3
    if pair:
        halo_ref, tail_ref = sources
        fill_pair(
            stage_ref,
            halo_ref,
            lambda f: tail_ref[f, 0:cols],
            lambda f: tail_ref[f, cols : cols + rows],
            lambda f: tail_ref[f, cols + rows : cols + rows + 1],
        )
    else:
        stage_ref[...] = sources[0][...].astype(jnp.float32)
    widen(stage_ref, window_ref)

    def put(at, value):
        rows_at = slice(at, at + value.shape[0])
        sum_ref[rows_at, :] = near_sum_ref[rows_at, :] + value

    for lag_t in range(extra):
        ahead = extra - lag_t
        pairs = [(t, t + ahead - frames) for t in range(frames) if t + ahead >= frames]
        tap_sums(
            act_ref, scale, pairs, lambda f: window_ref.at[f], (rows, cols, channels), lag_t, put
        )
    done = extra * 9 * channels
    sum_ref[done:, :] = near_sum_ref[done:, :]
    if not halves:
        outs[0][...] = sum_ref[...]
        return
    mine_ref, theirs_ref = outs
    col_side = lax.axis_index("width")
    half = rows_out // 2

    def place(low_ref, high_ref):
        for block in range(mine_ref.shape[0]):
            at = block * rows_out
            low_ref[block] = sum_ref[at : at + half, :]
            high_ref[block] = sum_ref[at + half : at + rows_out, :]

    @pl.when(col_side == 0)
    def _():
        place(mine_ref, theirs_ref)

    @pl.when(col_side == 1)
    def _():
        place(theirs_ref, mine_ref)


def conv_kernel(
    near_ref,
    far_ref,
    weight_ref,
    future_ref,
    features_ref,
    params_ref,
    scaled_ref,
    sums_ref,
):
    frames, rows, cols, channels = features_ref.shape
    cells = rows * cols
    wide = 3 * channels
    mean = params_ref[0:frames]
    rstd = params_ref[frames : 2 * frames]
    gain = params_ref[2 * frames : 2 * frames + 1]
    bias = params_ref[2 * frames + 1 : 2 * frames + 2]
    is_last = lax.axis_index("tm") == lax.axis_size("tm") - 1
    for t in range(frames):
        acc = None
        for lag_t in range(3):
            for lag_h in range(3):
                f = t + far_ref.shape[0] - lag_t
                source = near_ref.at[f] if f < frames else far_ref.at[f - frames]
                window = source[2 - lag_h : 2 - lag_h + rows]
                taps = jnp.concatenate(
                    [weight_ref[lag_t, lag_h, 2 - e] for e in range(3)], axis=1
                )
                term = lax.dot_general(
                    window.reshape(cells, wide),
                    taps,
                    (((1,), (1,)), ((), ())),
                    preferred_element_type=jnp.float32,
                )
                acc = term if acc is None else acc + term
        later = t - (frames - future_ref.shape[0])
        if later >= 0:
            tail = future_ref[later].astype(jnp.float32).reshape(cells, channels)
            acc = acc + jnp.where(is_last, tail, jnp.zeros_like(tail))
        value = features_ref[t].astype(jnp.float32).reshape(cells, channels)
        centred = (value - mean[t : t + 1]) * rstd[t : t + 1]
        pre_act = centred * gain + bias
        sig = jax.nn.sigmoid(pre_act)
        scaled = acc * sig * (1.0 + pre_act * (1.0 - sig)) * gain
        scaled_ref[t] = scaled.reshape(rows, cols, channels)
        sums_ref[t : t + 1, :] = jnp.sum(scaled, axis=0, keepdims=True)
        sums_ref[frames + t : frames + t + 1, :] = jnp.sum(
            scaled * centred, axis=0, keepdims=True
        )


def final_kernel(groups, count, terms, *refs):
    parts, (scaled_ref, features_ref, grad_ref, params_ref, out_ref) = refs[:terms], refs[terms:]
    frames, _, _, channels = features_ref.shape
    mean = params_ref[0:frames]
    rstd = params_ref[frames : 2 * frames]
    total = parts[0][...]
    for part in parts[1:]:
        total = total + part[...]
    width = channels // groups
    means = exact_dot(total, group_matrix(channels, channels, width, width)) / count
    for t in range(frames):
        value = features_ref[t].astype(jnp.float32)
        centred = (value - mean[t : t + 1]) * rstd[t : t + 1]
        first = means[t : t + 1]
        second = means[frames + t : frames + t + 1]
        corrected = rstd[t : t + 1] * (scaled_ref[t] - first - centred * second)
        out_ref[t] = (grad_ref[t].astype(jnp.float32) + corrected).astype(jnp.bfloat16)


def call(kernel, out_shape, scratch=(), flops=0, moved=0, in_specs=None, out_specs=None):
    here = pl.BlockSpec(memory_space=pltpu.VMEM)

    def run(*args):
        return pl.pallas_call(
            kernel,
            out_shape=out_shape,
            in_specs=in_specs or [here] * len(args),
            out_specs=out_specs or jax.tree.map(lambda _: here, out_shape),
            scratch_shapes=list(scratch),
            compiler_params=pltpu.CompilerParams(vmem_limit_bytes=VMEM_BYTES),
            cost_estimate=pl.CostEstimate(flops=flops, bytes_accessed=moved, transcendentals=0),
        )(*args)

    return run


def extended(cells, sides, width):
    for axis, dim in sides:
        head = lax.slice_in_dim(cells, 0, width, axis=dim)
        tail = lax.slice_in_dim(cells, cells.shape[dim] - width, cells.shape[dim], axis=dim)
        cells = jnp.concatenate(
            [shifted(tail, axis, 1), cells, shifted(head, axis, -1)], axis=dim
        )
    return cells


def rims(grad_out, extra):
    frames, rows, cols, channels = grad_out.shape

    def piece(*shape):
        return jax.ShapeDtypeStruct((*shape, channels), grad_out.dtype)

    halo, row, col, corner = call(
        cut_kernel,
        (piece(extra, rows, cols), piece(frames, cols), piece(frames, rows), piece(frames)),
    )(grad_out)
    halo = shifted(halo, "tm", -1)
    row = exchanged(row, "height", 1)
    corner = lax.ppermute(corner, ("height", "width"), [(i, 3 - i) for i in range(4)])
    col = exchanged(col, "width", 1)
    packed = call(pack_kernel, piece(extra, cols + rows + 1))(row, col, corner)
    tail = shifted(packed, "tm", -1)
    return (grad_out, row, col, corner), (halo, tail)


def on_device(features, grad_out, mean_saved, rstd_saved, gain, bias, weight, future_cot):
    frames, rows, cols, channels = features.shape
    extra = weight.shape[0] - 1
    cells = rows * cols
    groups = mean_saved.shape[1]
    blocks = lax.axis_size("tm")
    taps = math.prod(weight.shape[:3])
    rows_out = taps * channels // blocks
    positions = cells * lax.axis_size("height") * lax.axis_size("width")
    grad_scale = 1.0 / math.sqrt(positions * frames * blocks)
    gain = gain.reshape(1, channels)
    bias = bias.reshape(1, channels)
    pair = paired()
    halves = in_halves(blocks, rows_out)
    f32 = jnp.float32

    if pair:
        near_sources, far_sources = rims(grad_out, extra)
    else:
        padded = extended(grad_out, (("height", 1), ("width", 2)), 1)
        sides = ((0, 0), (0, 0), (LEAD - 1, LEAD - 1), (0, 0))
        near_sources = (jnp.pad(padded, sides),)
        far_sources = (jnp.pad(shifted(padded[:extra], "tm", -1), sides),)

    inputs = (features, mean_saved, rstd_saved, gain, bias)
    act, params = call(
        act_kernel,
        (
            jax.ShapeDtypeStruct((channels, frames * cells), jnp.bfloat16),
            jax.ShapeDtypeStruct((2 * frames + 2, channels), f32),
        ),
        scratch=(
            *[pltpu.VMEM(value.shape, value.dtype) for value in inputs],
            pltpu.SemaphoreType.DMA((len(inputs),)),
        ),
        in_specs=[pl.BlockSpec(memory_space=pltpu.HBM)] * len(inputs),
        flops=20 * frames * cells * channels,
        moved=4 * frames * cells * channels,
    )(*inputs)

    def window_shape(count):
        return jax.ShapeDtypeStruct((count, rows + 2, cols, 3 * channels), jnp.bfloat16)

    def stage_shape(count):
        return pltpu.VMEM((count, rows + 2, cols + 2 * LEAD, channels), f32)

    work = 2 * taps * channels * channels * frames * cells
    sum_shape = jax.ShapeDtypeStruct((taps * channels, channels), f32)
    near_window, near_sum = call(
        functools.partial(near_kernel, grad_scale, pair, extra),
        (window_shape(frames), sum_shape),
        scratch=(stage_shape(frames),),
        flops=3 * work // 4,
        moved=4 * 1024 * 1024,
    )(act, *near_sources)

    if halves:
        half_shape = jax.ShapeDtypeStruct((blocks, rows_out // 2, channels), f32)
        sum_shapes = (half_shape, half_shape)
    else:
        sum_shapes = (sum_shape,)
    far_window, *sums = call(
        functools.partial(far_kernel, rows_out, grad_scale, pair, halves, frames),
        (window_shape(extra), *sum_shapes),
        scratch=(stage_shape(extra), pltpu.VMEM((taps * channels, channels), f32)),
        flops=work // 4,
        moved=4 * 1024 * 1024,
    )(act, near_sum, *far_sources)

    if halves:
        weight_grad = reduced_share(*sums, rows_out)
    else:
        share = lax.psum_scatter(sums[0], "tm", scatter_dimension=0, tiled=True)
        weight_grad = lax.psum(share, ("height", "width"))

    scaled, local = call(
        conv_kernel,
        (
            jax.ShapeDtypeStruct((frames, rows, cols, channels), f32),
            jax.ShapeDtypeStruct((2 * frames, channels), f32),
        ),
        flops=work,
        moved=8 * 1024 * 1024,
    )(near_window, far_window, weight, future_cot, features, params)

    if pair:
        parts = [local]
        parts.append(exchanged(local, "width", 1))
        parts.append(exchanged(local, "height", 1))
        parts.append(
            lax.ppermute(local, ("height", "width"), [(i, 3 - i) for i in range(4)])
        )
    else:
        parts = [lax.psum(local, ("height", "width"))]
    input_cot = call(
        functools.partial(final_kernel, groups, positions * (channels // groups), len(parts)),
        jax.ShapeDtypeStruct(features.shape, jnp.bfloat16),
        flops=20 * frames * cells * channels,
        moved=10 * frames * cells * channels,
        out_specs=pl.BlockSpec(features.shape, lambda: (0, 0, 0, 0)),
    )(*parts, scaled, features, grad_out, params)
    return (input_cot, weight_grad)


def solution(mesh):
    placed = (
        P("tm", "height", "width", None),
        P("tm", "height", "width", None),
        P("tm", None),
        P("tm", None),
        P(),
        P(),
        P(),
        P(None, "height", "width", None),
    )
    return jax.shard_map(
        on_device,
        mesh=mesh,
        in_specs=placed,
        out_specs=(P("tm", "height", "width", None), P("tm", None)),
        check_vma=False,
    )
```

```python
import functools
import math

import jax
import jax.numpy as jnp
from jax import lax
from jax.experimental import pallas as pl
from jax.experimental.pallas import tpu as pltpu
from jax.sharding import PartitionSpec as P


LEAD = 8
VMEM_BYTES = 12 * 1024 * 1024


def exchanged(value, axis, distance):
    count = lax.axis_size(axis)
    return lax.ppermute(value, axis, [(i, i ^ distance) for i in range(count)])


def shifted(value, axis, steps):
    count = lax.axis_size(axis)
    initial, last = (max(0, -steps), min(count, count - steps))
    return lax.ppermute(value, axis, [(source, source + steps) for source in range(initial, last)])


def power_of_two(count):
    return count & (count - 1) == 0


def paired():
    return lax.axis_size("height") == 2 and lax.axis_size("width") == 2


def kept_rows(rows):
    return -(-rows // 16) * 8


def in_halves(blocks, rows):
    return paired() and power_of_two(blocks) and blocks >= 8 and rows % 16 == 0


def store_rows(value, near_ref, far_ref, at, side):
    rows, kept = value.shape[0], near_ref.shape[1]

    @pl.when(side == 0)
    def _():
        near_ref[at] = value[:kept]
        far_ref[at] = value[rows - kept :].astype(far_ref.dtype)

    @pl.when(side == 1)
    def _():
        near_ref[at] = value[rows - kept :]
        far_ref[at] = value[:kept].astype(far_ref.dtype)


def first_kernel(mine_ref, got_ref, rows_near_ref, rows_far_ref, pair_near_ref, pair_far_ref):
    low = rows_near_ref.shape[0]
    row_side = lax.axis_index("height")
    side = lax.axis_index("tm") % 2
    for block in range(low):
        value = mine_ref[block] + got_ref[block]
        store_rows(value, rows_near_ref, rows_far_ref, block, row_side)
    for pair in range(pair_near_ref.shape[0]):
        at = low + 2 * pair + side
        pair_near_ref[pair] = mine_ref[at] + got_ref[at]
        at = low + 2 * pair + 1 - side
        pair_far_ref[pair] = (mine_ref[at] + got_ref[at]).astype(pair_far_ref.dtype)


def second_kernel(
    rows_ref, rows_got_ref, pair_ref, pair_got_ref, low_near, low_far, high_near, high_far
):
    row_side = lax.axis_index("height")
    side = lax.axis_index("tm") % 2
    for pair in range(low_near.shape[0]):
        at = 2 * pair + side
        low_near[pair] = rows_ref[at] + rows_got_ref[at].astype(jnp.float32)
        at = 2 * pair + 1 - side
        low_far[pair] = (rows_ref[at] + rows_got_ref[at].astype(jnp.float32)).astype(low_far.dtype)
        value = pair_ref[pair] + pair_got_ref[pair].astype(jnp.float32)
        store_rows(value, high_near, high_far, pair, row_side)


def split_kernel(distance, low, *refs):
    *parts, near_ref, far_ref = refs
    side = (lax.axis_index("tm") // distance) % 2

    def block(pair, which):
        at = 2 * pair + which
        if 2 * pair < low:
            value_ref, got_ref = parts[:2]
        else:
            value_ref, got_ref = parts[-2:]
            at = at - low
        return value_ref[at] + got_ref[at].astype(jnp.float32)

    for pair in range(near_ref.shape[0]):
        near_ref[pair] = block(pair, side)
        far_ref[pair] = block(pair, 1 - side).astype(far_ref.dtype)


def add_kernel(near_ref, got_ref, out_ref):
    out_ref[...] = near_ref[0] + got_ref[0].astype(jnp.float32)


def half_kernel(own_ref, below_ref, out_ref):
    kept, half = own_ref.shape[0], out_ref.shape[0]

    def place(low_ref, high_ref):
        out_ref[:kept, :] = low_ref[...]
        out_ref[kept:, :] = high_ref[2 * kept - half :, :]

    @pl.when(lax.axis_index("height") == 0)
    def _():
        place(own_ref, below_ref)

    @pl.when(lax.axis_index("height") == 1)
    def _():
        place(below_ref, own_ref)


def whole_kernel(own_ref, beside_ref, out_ref):
    half = own_ref.shape[0]
    side = lax.axis_index("width")
    out_ref[pl.ds(pl.multiple_of(side * half, 8), half), :] = own_ref[...]
    out_ref[pl.ds(pl.multiple_of((1 - side) * half, 8), half), :] = beside_ref[...]


def reduced_share(mine, theirs, rows):
    blocks, half, channels = mine.shape
    kept = kept_rows(half)
    f32, wire = jnp.float32, jnp.bfloat16

    def both(count, high):
        return tuple(jax.ShapeDtypeStruct((count, high, channels), kind) for kind in (f32, wire))

    got = exchanged(theirs, "width", 1)
    low, pairs = blocks // 2, blocks // 4
    near_rows, far_rows, near_pair, far_pair = call(
        first_kernel, (*both(low, kept), *both(pairs, half))
    )(mine, got)
    got_rows = exchanged(far_rows, "height", 1)
    got_pair = exchanged(far_pair, "tm", 1)
    near_low, far_low, near_high, far_high = call(
        second_kernel, (*both(pairs, kept), *both(pairs, kept))
    )(near_rows, got_rows, near_pair, got_pair)
    got_low = exchanged(far_low, "tm", 1)
    got_high = exchanged(far_high, "height", 1)
    parts = (near_low, got_low, near_high, got_high)
    low, distance = pairs, 2
    while distance < blocks:
        count = blocks // distance // 2
        near, far = call(functools.partial(split_kernel, distance, low), both(count, kept))(*parts)
        parts = (near, exchanged(far, "tm", distance))
        low = count
        distance *= 2
    own = call(add_kernel, jax.ShapeDtypeStruct((kept, channels), f32))(*parts)
    below = exchanged(own, "height", 1)
    own = call(half_kernel, jax.ShapeDtypeStruct((half, channels), f32))(own, below)
    beside = exchanged(own, "width", 1)
    return call(
        whole_kernel,
        jax.ShapeDtypeStruct((rows, channels), f32),
        out_specs=pl.BlockSpec((rows, channels), lambda: (0, 0)),
    )(own, beside)


def group_matrix(rows, cols, row_width, col_width):
    row = lax.broadcasted_iota(jnp.int32, (rows, cols), 0) // row_width
    col = lax.broadcasted_iota(jnp.int32, (rows, cols), 1) // col_width
    return (row == col).astype(jnp.float32)


def exact_dot(left, right):
    return lax.dot_general(
        left,
        right,
        (((1,), (0,)), ((), ())),
        precision=lax.Precision.HIGHEST,
        preferred_element_type=jnp.float32,
    )


def per_channel(value, channels):
    groups = value.shape[1]
    return exact_dot(value, group_matrix(groups, channels, 1, channels // groups))


def cut_kernel(grad_ref, halo_ref, row_ref, col_ref, corner_ref, copy_ref):
    frames, rows, cols, _ = grad_ref.shape
    copy_ref[...] = grad_ref[...]
    halo_ref[...] = grad_ref[: halo_ref.shape[0]]
    row_at = (1 - lax.axis_index("height")) * (rows - 1)

    def columns(at):
        corners = []
        for f in range(frames):
            col_ref[f] = grad_ref[f].astype(jnp.float32)[:, at].astype(jnp.bfloat16)
            corners.append(grad_ref[f, row_at].astype(jnp.float32)[at : at + 1])
        corner_ref[...] = jnp.concatenate(corners, axis=0).astype(jnp.bfloat16)

    for f in range(frames):
        row_ref[f] = grad_ref[f, row_at]

    @pl.when(lax.axis_index("width") == 0)
    def _():
        columns(cols - 1)

    @pl.when(lax.axis_index("width") == 1)
    def _():
        columns(0)


def pack_kernel(row_ref, col_ref, corner_ref, tail_ref):
    cols, rows = row_ref.shape[1], col_ref.shape[1]
    for f in range(tail_ref.shape[0]):
        tail_ref[f, 0:cols] = row_ref[f]
        tail_ref[f, cols : cols + rows] = col_ref[f]
        tail_ref[f, cols + rows :] = corner_ref[f : f + 1]


def act_kernel(features_hbm, mean_hbm, rstd_hbm, gain_hbm, bias_hbm, act_ref, params_ref, *scratch):
    buffers, sems = scratch[:5], scratch[5]
    sources = (features_hbm, mean_hbm, rstd_hbm, gain_hbm, bias_hbm)
    copies = [
        pltpu.make_async_copy(source, buffer, sems.at[i])
        for i, (source, buffer) in enumerate(zip(sources, buffers))
    ]
    for copy in copies:
        copy.start()
    for copy in copies:
        copy.wait()
    features_ref, mean_ref, rstd_ref, gain_ref, bias_ref = buffers
    frames, rows, cols, channels = features_ref.shape
    cells = rows * cols
    mean = per_channel(mean_ref[...], channels)
    rstd = per_channel(rstd_ref[...], channels)
    gain, bias = gain_ref[...], bias_ref[...]
    params_ref[...] = jnp.concatenate([mean, rstd, gain, bias], axis=0)
    for t in range(frames):
        value = features_ref[t].astype(jnp.float32).reshape(cells, channels)
        centred = (value - mean[t : t + 1]) * rstd[t : t + 1]
        pre_act = centred * gain + bias
        act = (pre_act * jax.nn.sigmoid(pre_act)).astype(jnp.bfloat16)
        act_ref[:, t * cells : (t + 1) * cells] = act.T


def fill_pair(stage_ref, inner_ref, row_of, col_of, corner_of):
    total, rows, cols, channels = inner_ref.shape
    row_side = lax.axis_index("height")
    col_side = lax.axis_index("width")
    rim_row = (1 - row_side) * (rows + 1)
    for f in range(total):
        zeros = jnp.zeros((rows + 2, LEAD, channels), jnp.float32)
        stage_ref[f, :, 0:LEAD, :] = zeros
        stage_ref[f, :, LEAD + cols :, :] = zeros
        empty = jnp.zeros((cols, channels), jnp.float32)
        stage_ref[f, 0, LEAD : LEAD + cols, :] = empty
        stage_ref[f, rows + 1, LEAD : LEAD + cols, :] = empty
        stage_ref[f, 1 : rows + 1, LEAD : LEAD + cols, :] = inner_ref[f].astype(jnp.float32)
        stage_ref[f, rim_row, LEAD : LEAD + cols, :] = row_of(f).astype(jnp.float32)

    def fill_columns(at):
        for f in range(total):
            column = col_of(f).astype(jnp.float32)
            for r in range(rows):
                stage_ref[f, r + 1, at : at + 1, :] = column[r : r + 1]
            stage_ref[f, rim_row, at : at + 1, :] = corner_of(f).astype(jnp.float32)

    @pl.when(col_side == 1)
    def _():
        fill_columns(LEAD - 1)

    @pl.when(col_side == 0)
    def _():
        fill_columns(LEAD + cols)


def widen(stage_ref, window_ref):
    total, _, cols, wide = window_ref.shape
    channels = wide // 3

    def one(f, carry):
        for e in range(3):
            at = LEAD - 1 + e
            window_ref[f, :, :, e * channels : (e + 1) * channels] = stage_ref[
                f, :, at : at + cols, :
            ].astype(jnp.bfloat16)
        return carry

    lax.fori_loop(0, total, one, 0)


def tap_sums(act_ref, scale, pairs, window_of, shape, lag_t, add):
    rows, cols, channels = shape
    cells = rows * cols
    for lag_h in range(3):
        acc = None
        for t, f in pairs:
            window = window_of(f)[2 - lag_h : 2 - lag_h + rows]
            term = lax.dot_general(
                act_ref[:, t * cells : (t + 1) * cells],
                window.reshape(cells, window.shape[-1]),
                (((1,), (0,)), ((), ())),
                preferred_element_type=jnp.float32,
            )
            acc = term if acc is None else acc + term
        for lag_w in range(3):
            e = 2 - lag_w
            at = ((lag_t * 3 + lag_h) * 3 + lag_w) * channels
            if acc is None:
                value = jnp.zeros((channels, channels), jnp.float32)
            else:
                value = scale * acc[:, e * channels : (e + 1) * channels]
            add(at, value)


def near_kernel(scale, pair, extra, act_ref, *refs):
    sources, (window_ref, sum_ref, stage_ref) = refs[:-3], refs[-3:]
    frames, rows_ext, cols, wide = window_ref.shape
    shape = (rows_ext - 2, cols, wide // 3)
    if pair:
        grad_ref, row_ref, col_ref, corner_ref = sources
        fill_pair(
            stage_ref,
            grad_ref,
            lambda f: row_ref[f],
            lambda f: col_ref[f],
            lambda f: corner_ref[f : f + 1],
        )
    else:
        stage_ref[...] = sources[0][...].astype(jnp.float32)
    widen(stage_ref, window_ref)

    def put(at, value):
        sum_ref[at : at + value.shape[0], :] = value

    for lag_t in range(extra + 1):
        ahead = extra - lag_t
        pairs = [(t, t + ahead) for t in range(frames) if t + ahead < frames]
        tap_sums(act_ref, scale, pairs, lambda f: window_ref.at[f], shape, lag_t, put)


def far_kernel(rows_out, scale, pair, halves, frames, act_ref, near_sum_ref, *refs):
    count = 2 if pair else 1
    sources, window_ref, outs, (stage_ref, sum_ref) = (
        refs[:count],
        refs[count],
        refs[count + 1 : -2],
        refs[-2:],
    )
    extra, rows_ext, cols, wide = window_ref.shape
    rows = rows_ext - 2
    channels = wide // 3
    if pair:
        halo_ref, tail_ref = sources
        fill_pair(
            stage_ref,
            halo_ref,
            lambda f: tail_ref[f, 0:cols],
            lambda f: tail_ref[f, cols : cols + rows],
            lambda f: tail_ref[f, cols + rows : cols + rows + 1],
        )
    else:
        stage_ref[...] = sources[0][...].astype(jnp.float32)
    widen(stage_ref, window_ref)

    def put(at, value):
        rows_at = slice(at, at + value.shape[0])
        sum_ref[rows_at, :] = near_sum_ref[rows_at, :] + value

    for lag_t in range(extra):
        ahead = extra - lag_t
        pairs = [(t, t + ahead - frames) for t in range(frames) if t + ahead >= frames]
        tap_sums(
            act_ref, scale, pairs, lambda f: window_ref.at[f], (rows, cols, channels), lag_t, put
        )
    done = extra * 9 * channels
    sum_ref[done:, :] = near_sum_ref[done:, :]
    if not halves:
        outs[0][...] = sum_ref[...]
        return
    mine_ref, theirs_ref = outs
    col_side = lax.axis_index("width")
    half = rows_out // 2

    def place(low_ref, high_ref):
        for block in range(mine_ref.shape[0]):
            at = block * rows_out
            low_ref[block] = sum_ref[at : at + half, :]
            high_ref[block] = sum_ref[at + half : at + rows_out, :]

    @pl.when(col_side == 0)
    def _():
        place(mine_ref, theirs_ref)

    @pl.when(col_side == 1)
    def _():
        place(theirs_ref, mine_ref)


def conv_kernel(
    near_ref,
    far_ref,
    weight_ref,
    future_ref,
    features_ref,
    params_ref,
    scaled_ref,
    sums_ref,
):
    frames, rows, cols, channels = features_ref.shape
    cells = rows * cols
    wide = 3 * channels
    mean = params_ref[0:frames]
    rstd = params_ref[frames : 2 * frames]
    gain = params_ref[2 * frames : 2 * frames + 1]
    bias = params_ref[2 * frames + 1 : 2 * frames + 2]
    is_last = lax.axis_index("tm") == lax.axis_size("tm") - 1
    for t in range(frames):
        acc = None
        for lag_t in range(3):
            for lag_h in range(3):
                f = t + far_ref.shape[0] - lag_t
                source = near_ref.at[f] if f < frames else far_ref.at[f - frames]
                window = source[2 - lag_h : 2 - lag_h + rows]
                taps = jnp.concatenate(
                    [weight_ref[lag_t, lag_h, 2 - e] for e in range(3)], axis=1
                )
                term = lax.dot_general(
                    window.reshape(cells, wide),
                    taps,
                    (((1,), (1,)), ((), ())),
                    preferred_element_type=jnp.float32,
                )
                acc = term if acc is None else acc + term
        later = t - (frames - future_ref.shape[0])
        if later >= 0:
            tail = future_ref[later].astype(jnp.float32).reshape(cells, channels)
            acc = acc + jnp.where(is_last, tail, jnp.zeros_like(tail))
        value = features_ref[t].astype(jnp.float32).reshape(cells, channels)
        centred = (value - mean[t : t + 1]) * rstd[t : t + 1]
        pre_act = centred * gain + bias
        sig = jax.nn.sigmoid(pre_act)
        scaled = acc * sig * (1.0 + pre_act * (1.0 - sig)) * gain
        scaled_ref[t] = scaled.reshape(rows, cols, channels)
        sums_ref[t : t + 1, :] = jnp.sum(scaled, axis=0, keepdims=True)
        sums_ref[frames + t : frames + t + 1, :] = jnp.sum(
            scaled * centred, axis=0, keepdims=True
        )


def final_kernel(groups, count, terms, *refs):
    parts, (scaled_ref, features_ref, grad_ref, params_ref, out_ref) = refs[:terms], refs[terms:]
    frames, _, _, channels = features_ref.shape
    mean = params_ref[0:frames]
    rstd = params_ref[frames : 2 * frames]
    total = parts[0][...]
    for part in parts[1:]:
        total = total + part[...]
    width = channels // groups
    means = exact_dot(total, group_matrix(channels, channels, width, width)) / count
    for t in range(frames):
        value = features_ref[t].astype(jnp.float32)
        centred = (value - mean[t : t + 1]) * rstd[t : t + 1]
        first = means[t : t + 1]
        second = means[frames + t : frames + t + 1]
        corrected = rstd[t : t + 1] * (scaled_ref[t] - first - centred * second)
        out_ref[t] = (grad_ref[t].astype(jnp.float32) + corrected).astype(jnp.bfloat16)


def call(kernel, out_shape, scratch=(), flops=0, moved=0, in_specs=None, out_specs=None):
    here = pl.BlockSpec(memory_space=pltpu.VMEM)

    def run(*args):
        return pl.pallas_call(
            kernel,
            out_shape=out_shape,
            in_specs=in_specs or [here] * len(args),
            out_specs=out_specs or jax.tree.map(lambda _: here, out_shape),
            scratch_shapes=list(scratch),
            compiler_params=pltpu.CompilerParams(vmem_limit_bytes=VMEM_BYTES),
            cost_estimate=pl.CostEstimate(flops=flops, bytes_accessed=moved, transcendentals=0),
        )(*args)

    return run


def extended(cells, sides, width):
    for axis, dim in sides:
        head = lax.slice_in_dim(cells, 0, width, axis=dim)
        tail = lax.slice_in_dim(cells, cells.shape[dim] - width, cells.shape[dim], axis=dim)
        cells = jnp.concatenate(
            [shifted(tail, axis, 1), cells, shifted(head, axis, -1)], axis=dim
        )
    return cells


def rims(grad_out, extra):
    frames, rows, cols, channels = grad_out.shape

    def piece(*shape):
        return jax.ShapeDtypeStruct((*shape, channels), grad_out.dtype)

    halo, row, col, corner, held = call(
        cut_kernel,
        (
            piece(extra, rows, cols),
            piece(frames, cols),
            piece(frames, rows),
            piece(frames),
            piece(frames, rows, cols),
        ),
    )(grad_out)
    halo = shifted(halo, "tm", -1)
    row = exchanged(row, "height", 1)
    corner = lax.ppermute(corner, ("height", "width"), [(i, 3 - i) for i in range(4)])
    col = exchanged(col, "width", 1)
    packed = call(pack_kernel, piece(extra, cols + rows + 1))(row, col, corner)
    tail = shifted(packed, "tm", -1)
    return (held, row, col, corner), (halo, tail)


def on_device(features, grad_out, mean_saved, rstd_saved, gain, bias, weight, future_cot):
    frames, rows, cols, channels = features.shape
    extra = weight.shape[0] - 1
    cells = rows * cols
    groups = mean_saved.shape[1]
    blocks = lax.axis_size("tm")
    taps = math.prod(weight.shape[:3])
    rows_out = taps * channels // blocks
    positions = cells * lax.axis_size("height") * lax.axis_size("width")
    grad_scale = 1.0 / math.sqrt(positions * frames * blocks)
    gain = gain.reshape(1, channels)
    bias = bias.reshape(1, channels)
    pair = paired()
    halves = in_halves(blocks, rows_out)
    f32 = jnp.float32

    if pair:
        near_sources, far_sources = rims(grad_out, extra)
    else:
        padded = extended(grad_out, (("height", 1), ("width", 2)), 1)
        sides = ((0, 0), (0, 0), (LEAD - 1, LEAD - 1), (0, 0))
        near_sources = (jnp.pad(padded, sides),)
        far_sources = (jnp.pad(shifted(padded[:extra], "tm", -1), sides),)

    inputs = tuple(
        pltpu.with_memory_space_constraint(value, pltpu.HBM)
        for value in (features, mean_saved, rstd_saved, gain, bias)
    )
    act, params = call(
        act_kernel,
        (
            jax.ShapeDtypeStruct((channels, frames * cells), jnp.bfloat16),
            jax.ShapeDtypeStruct((2 * frames + 2, channels), f32),
        ),
        scratch=(
            *[pltpu.VMEM(value.shape, value.dtype) for value in inputs],
            pltpu.SemaphoreType.DMA((len(inputs),)),
        ),
        in_specs=[pl.BlockSpec(memory_space=pltpu.HBM)] * len(inputs),
        flops=20 * frames * cells * channels,
        moved=4 * frames * cells * channels,
    )(*inputs)

    def window_shape(count):
        return jax.ShapeDtypeStruct((count, rows + 2, cols, 3 * channels), jnp.bfloat16)

    def stage_shape(count):
        return pltpu.VMEM((count, rows + 2, cols + 2 * LEAD, channels), f32)

    work = 2 * taps * channels * channels * frames * cells
    sum_shape = jax.ShapeDtypeStruct((taps * channels, channels), f32)
    near_window, near_sum = call(
        functools.partial(near_kernel, grad_scale, pair, extra),
        (window_shape(frames), sum_shape),
        scratch=(stage_shape(frames),),
        flops=3 * work // 4,
        moved=4 * 1024 * 1024,
    )(act, *near_sources)

    if halves:
        half_shape = jax.ShapeDtypeStruct((blocks, rows_out // 2, channels), f32)
        sum_shapes = (half_shape, half_shape)
    else:
        sum_shapes = (sum_shape,)
    far_window, *sums = call(
        functools.partial(far_kernel, rows_out, grad_scale, pair, halves, frames),
        (window_shape(extra), *sum_shapes),
        scratch=(stage_shape(extra), pltpu.VMEM((taps * channels, channels), f32)),
        flops=work // 4,
        moved=4 * 1024 * 1024,
    )(act, near_sum, *far_sources)

    if halves:
        weight_grad = reduced_share(*sums, rows_out)
    else:
        share = lax.psum_scatter(sums[0], "tm", scatter_dimension=0, tiled=True)
        weight_grad = lax.psum(share, ("height", "width"))

    scaled, local = call(
        conv_kernel,
        (
            jax.ShapeDtypeStruct((frames, rows, cols, channels), f32),
            jax.ShapeDtypeStruct((2 * frames, channels), f32),
        ),
        flops=work,
        moved=8 * 1024 * 1024,
    )(near_window, far_window, weight, future_cot, features, params)

    if pair:
        parts = [local]
        parts.append(exchanged(local, "width", 1))
        parts.append(exchanged(local, "height", 1))
        parts.append(
            lax.ppermute(local, ("height", "width"), [(i, 3 - i) for i in range(4)])
        )
    else:
        parts = [lax.psum(local, ("height", "width"))]
    input_cot = call(
        functools.partial(final_kernel, groups, positions * (channels // groups), len(parts)),
        jax.ShapeDtypeStruct(features.shape, jnp.bfloat16),
        flops=20 * frames * cells * channels,
        moved=10 * frames * cells * channels,
        out_specs=pl.BlockSpec(features.shape, lambda: (0, 0, 0, 0)),
    )(*parts, scaled, features, grad_out, params)
    return (input_cot, weight_grad)


def solution(mesh):
    placed = (
        P("tm", "height", "width", None),
        P("tm", "height", "width", None),
        P("tm", None),
        P("tm", None),
        P(),
        P(),
        P(),
        P(None, "height", "width", None),
    )
    return jax.shard_map(
        on_device,
        mesh=mesh,
        in_specs=placed,
        out_specs=(P("tm", "height", "width", None), P("tm", None)),
        check_vma=False,
    )
```

```python
import functools
import math

import jax
import jax.numpy as jnp
from jax import lax
from jax.experimental import pallas as pl
from jax.experimental.pallas import tpu as pltpu
from jax.sharding import PartitionSpec as P


LEAD = 8
VMEM_BYTES = 12 * 1024 * 1024


def exchanged(value, axis, distance):
    count = lax.axis_size(axis)
    return lax.ppermute(value, axis, [(i, i ^ distance) for i in range(count)])


def shifted(value, axis, steps):
    count = lax.axis_size(axis)
    initial, last = (max(0, -steps), min(count, count - steps))
    return lax.ppermute(value, axis, [(source, source + steps) for source in range(initial, last)])


def power_of_two(count):
    return count & (count - 1) == 0


def paired():
    return lax.axis_size("height") == 2 and lax.axis_size("width") == 2


def in_halves(blocks, rows):
    return paired() and power_of_two(blocks) and blocks >= 8 and rows % 16 == 0


def tm_side(distance):
    return (lax.axis_index("tm") // distance) % 2


def first_kernel(mine_ref, got_ref, low_near, low_far, high_near, high_far):
    half = mine_ref.shape[0] // 2
    near_side, next_side = tm_side(1), tm_side(2)

    def block(at):
        return mine_ref[at] + got_ref[at]

    for i in range(low_near.shape[0]):
        low_near[i] = block(2 * i + near_side)
        low_far[i] = block(2 * i + 1 - near_side).astype(low_far.dtype)
    for i in range(high_near.shape[0]):
        at = half + 4 * (i // 2) + i % 2
        high_near[i] = block(at + 2 * next_side)
        high_far[i] = block(at + 2 * (1 - next_side)).astype(high_far.dtype)


def second_kernel(low_ref, low_got_ref, high_ref, high_got_ref, *outs):
    low_near, low_far, high_near, high_far = outs

    def halve(value_ref, got_ref, near_ref, far_ref, side):
        for i in range(near_ref.shape[0]):
            at = 2 * i + side
            near_ref[i] = value_ref[at] + got_ref[at].astype(jnp.float32)
            at = 2 * i + 1 - side
            value = value_ref[at] + got_ref[at].astype(jnp.float32)
            far_ref[i] = value.astype(far_ref.dtype)

    halve(low_ref, low_got_ref, low_near, low_far, tm_side(2))
    halve(high_ref, high_got_ref, high_near, high_far, tm_side(1))


def split_kernel(distance, *refs):
    *parts, near_ref, far_ref = refs
    blocks = [
        (value_ref, got_ref, at)
        for value_ref, got_ref in zip(parts[::2], parts[1::2])
        for at in range(value_ref.shape[0])
    ]

    def block(i):
        value_ref, got_ref, at = blocks[i]
        return value_ref[at] + got_ref[at].astype(jnp.float32)

    for which in range(2):

        @pl.when(tm_side(distance) == which)
        def _():
            for i in range(near_ref.shape[0]):
                near_ref[i] = block(2 * i + which)
                far_ref[i] = block(2 * i + 1 - which).astype(far_ref.dtype)


def add_kernel(own_ref, got_ref, out_ref):
    out_ref[...] = own_ref[...] + got_ref[...].astype(jnp.float32)


def whole_kernel(own_ref, got_ref, beside_ref, out_ref):
    half = own_ref.shape[1]
    side = lax.axis_index("width")
    mine = pl.multiple_of(side * half, 8)
    other = pl.multiple_of((1 - side) * half, 8)
    out_ref[pl.ds(mine, half), :] = own_ref[0] + got_ref[0]
    out_ref[pl.ds(other, half), :] = beside_ref[0]


def reduced_share(mine, theirs, rows):
    blocks, half, channels = mine.shape
    f32, wire = jnp.float32, jnp.bfloat16

    def both(count):
        return tuple(jax.ShapeDtypeStruct((count, half, channels), kind) for kind in (f32, wire))

    got = exchanged(theirs, "width", 1)
    low, low_far, high, high_far = call(
        first_kernel, (*both(blocks // 4), *both(blocks // 4))
    )(mine, got)
    low_got = exchanged(low_far, "tm", 1)
    high_got = exchanged(high_far, "tm", 2)
    low, low_far, high, high_far = call(
        second_kernel, (*both(blocks // 8), *both(blocks // 8))
    )(low, low_got, high, high_got)
    low_got = exchanged(low_far, "tm", 2)
    high_got = exchanged(high_far, "tm", 1)
    parts = (low, low_got, high, high_got)
    distance = 4
    while distance < blocks:
        near, far = call(
            functools.partial(split_kernel, distance), both(blocks // distance // 2)
        )(*parts)
        parts = (near, exchanged(far, "tm", distance))
        distance *= 2
    share = both(1)[0]
    own = call(add_kernel, share)(*parts)
    got = exchanged(own, "height", 1)
    total = call(add_kernel, share)(own, got)
    beside = exchanged(total, "width", 1)
    return call(
        whole_kernel,
        jax.ShapeDtypeStruct((rows, channels), f32),
        out_specs=pl.BlockSpec((rows, channels), lambda: (0, 0)),
    )(own, got, beside)


def group_matrix(rows, cols, row_width, col_width):
    row = lax.broadcasted_iota(jnp.int32, (rows, cols), 0) // row_width
    col = lax.broadcasted_iota(jnp.int32, (rows, cols), 1) // col_width
    return (row == col).astype(jnp.float32)


def exact_dot(left, right):
    return lax.dot_general(
        left,
        right,
        (((1,), (0,)), ((), ())),
        precision=lax.Precision.HIGHEST,
        preferred_element_type=jnp.float32,
    )


def per_channel(value, channels):
    groups = value.shape[1]
    return exact_dot(value, group_matrix(groups, channels, 1, channels // groups))


def cut_kernel(grad_ref, halo_ref, row_ref, col_ref, corner_ref, copy_ref):
    frames, rows, cols, _ = grad_ref.shape
    copy_ref[...] = grad_ref[...]
    halo_ref[...] = grad_ref[: halo_ref.shape[0]]
    row_at = (1 - lax.axis_index("height")) * (rows - 1)

    def columns(at):
        corners = []
        for f in range(frames):
            col_ref[f] = grad_ref[f].astype(jnp.float32)[:, at].astype(jnp.bfloat16)
            corners.append(grad_ref[f, row_at].astype(jnp.float32)[at : at + 1])
        corner_ref[...] = jnp.concatenate(corners, axis=0).astype(jnp.bfloat16)

    for f in range(frames):
        row_ref[f] = grad_ref[f, row_at]

    @pl.when(lax.axis_index("width") == 0)
    def _():
        columns(cols - 1)

    @pl.when(lax.axis_index("width") == 1)
    def _():
        columns(0)


def pack_kernel(row_ref, col_ref, corner_ref, tail_ref):
    cols, rows = row_ref.shape[1], col_ref.shape[1]
    for f in range(tail_ref.shape[0]):
        tail_ref[f, 0:cols] = row_ref[f]
        tail_ref[f, cols : cols + rows] = col_ref[f]
        tail_ref[f, cols + rows :] = corner_ref[f : f + 1]


def act_kernel(features_hbm, mean_hbm, rstd_hbm, gain_hbm, bias_hbm, act_ref, params_ref, *scratch):
    buffers, sems = scratch[:5], scratch[5]
    sources = (features_hbm, mean_hbm, rstd_hbm, gain_hbm, bias_hbm)
    copies = [
        pltpu.make_async_copy(source, buffer, sems.at[i])
        for i, (source, buffer) in enumerate(zip(sources, buffers))
    ]
    for copy in copies:
        copy.start()
    for copy in copies:
        copy.wait()
    features_ref, mean_ref, rstd_ref, gain_ref, bias_ref = buffers
    frames, rows, cols, channels = features_ref.shape
    cells = rows * cols
    mean = per_channel(mean_ref[...], channels)
    rstd = per_channel(rstd_ref[...], channels)
    gain, bias = gain_ref[...], bias_ref[...]
    params_ref[...] = jnp.concatenate([mean, rstd, gain, bias], axis=0)
    for t in range(frames):
        value = features_ref[t].astype(jnp.float32).reshape(cells, channels)
        centred = (value - mean[t : t + 1]) * rstd[t : t + 1]
        pre_act = centred * gain + bias
        act = (pre_act * jax.nn.sigmoid(pre_act)).astype(jnp.bfloat16)
        act_ref[:, t * cells : (t + 1) * cells] = act.T


def fill_pair(stage_ref, inner_ref, row_of, col_of, corner_of):
    total, rows, cols, channels = inner_ref.shape
    row_side = lax.axis_index("height")
    col_side = lax.axis_index("width")
    rim_row = (1 - row_side) * (rows + 1)
    for f in range(total):
        zeros = jnp.zeros((rows + 2, LEAD, channels), jnp.float32)
        stage_ref[f, :, 0:LEAD, :] = zeros
        stage_ref[f, :, LEAD + cols :, :] = zeros
        empty = jnp.zeros((cols, channels), jnp.float32)
        stage_ref[f, 0, LEAD : LEAD + cols, :] = empty
        stage_ref[f, rows + 1, LEAD : LEAD + cols, :] = empty
        stage_ref[f, 1 : rows + 1, LEAD : LEAD + cols, :] = inner_ref[f].astype(jnp.float32)
        stage_ref[f, rim_row, LEAD : LEAD + cols, :] = row_of(f).astype(jnp.float32)

    def fill_columns(at):
        for f in range(total):
            column = col_of(f).astype(jnp.float32)
            for r in range(rows):
                stage_ref[f, r + 1, at : at + 1, :] = column[r : r + 1]
            stage_ref[f, rim_row, at : at + 1, :] = corner_of(f).astype(jnp.float32)

    @pl.when(col_side == 1)
    def _():
        fill_columns(LEAD - 1)

    @pl.when(col_side == 0)
    def _():
        fill_columns(LEAD + cols)


def widen(stage_ref, window_ref):
    total, _, cols, wide = window_ref.shape
    channels = wide // 3

    def one(f, carry):
        for e in range(3):
            at = LEAD - 1 + e
            window_ref[f, :, :, e * channels : (e + 1) * channels] = stage_ref[
                f, :, at : at + cols, :
            ].astype(jnp.bfloat16)
        return carry

    lax.fori_loop(0, total, one, 0)


def tap_sums(act_ref, scale, pairs, window_of, shape, lag_t, add):
    rows, cols, channels = shape
    cells = rows * cols
    for lag_h in range(3):
        acc = None
        for t, f in pairs:
            window = window_of(f)[2 - lag_h : 2 - lag_h + rows]
            term = lax.dot_general(
                act_ref[:, t * cells : (t + 1) * cells],
                window.reshape(cells, window.shape[-1]),
                (((1,), (0,)), ((), ())),
                preferred_element_type=jnp.float32,
            )
            acc = term if acc is None else acc + term
        for lag_w in range(3):
            e = 2 - lag_w
            at = ((lag_t * 3 + lag_h) * 3 + lag_w) * channels
            if acc is None:
                value = jnp.zeros((channels, channels), jnp.float32)
            else:
                value = scale * acc[:, e * channels : (e + 1) * channels]
            add(at, value)


def near_kernel(scale, pair, extra, act_ref, *refs):
    sources, (window_ref, sum_ref, stage_ref) = refs[:-3], refs[-3:]
    frames, rows_ext, cols, wide = window_ref.shape
    shape = (rows_ext - 2, cols, wide // 3)
    if pair:
        grad_ref, row_ref, col_ref, corner_ref = sources
        fill_pair(
            stage_ref,
            grad_ref,
            lambda f: row_ref[f],
            lambda f: col_ref[f],
            lambda f: corner_ref[f : f + 1],
        )
    else:
        stage_ref[...] = sources[0][...].astype(jnp.float32)
    widen(stage_ref, window_ref)

    def put(at, value):
        sum_ref[at : at + value.shape[0], :] = value

    for lag_t in range(extra + 1):
        ahead = extra - lag_t
        pairs = [(t, t + ahead) for t in range(frames) if t + ahead < frames]
        tap_sums(act_ref, scale, pairs, lambda f: window_ref.at[f], shape, lag_t, put)


def far_kernel(rows_out, scale, pair, halves, frames, act_ref, near_sum_ref, *refs):
    count = 2 if pair else 1
    sources, window_ref, outs, (stage_ref, sum_ref) = (
        refs[:count],
        refs[count],
        refs[count + 1 : -2],
        refs[-2:],
    )
    extra, rows_ext, cols, wide = window_ref.shape
    rows = rows_ext - 2
    channels = wide // 3
    if pair:
        halo_ref, tail_ref = sources
        fill_pair(
            stage_ref,
            halo_ref,
            lambda f: tail_ref[f, 0:cols],
            lambda f: tail_ref[f, cols : cols + rows],
            lambda f: tail_ref[f, cols + rows : cols + rows + 1],
        )
    else:
        stage_ref[...] = sources[0][...].astype(jnp.float32)
    widen(stage_ref, window_ref)

    def put(at, value):
        rows_at = slice(at, at + value.shape[0])
        sum_ref[rows_at, :] = near_sum_ref[rows_at, :] + value

    for lag_t in range(extra):
        ahead = extra - lag_t
        pairs = [(t, t + ahead - frames) for t in range(frames) if t + ahead >= frames]
        tap_sums(
            act_ref, scale, pairs, lambda f: window_ref.at[f], (rows, cols, channels), lag_t, put
        )
    done = extra * 9 * channels
    sum_ref[done:, :] = near_sum_ref[done:, :]
    if not halves:
        outs[0][...] = sum_ref[...]
        return
    mine_ref, theirs_ref = outs
    col_side = lax.axis_index("width")
    half = rows_out // 2

    def place(low_ref, high_ref):
        for block in range(mine_ref.shape[0]):
            at = block * rows_out
            low_ref[block] = sum_ref[at : at + half, :]
            high_ref[block] = sum_ref[at + half : at + rows_out, :]

    @pl.when(col_side == 0)
    def _():
        place(mine_ref, theirs_ref)

    @pl.when(col_side == 1)
    def _():
        place(theirs_ref, mine_ref)


def conv_kernel(
    near_ref,
    far_ref,
    weight_ref,
    future_ref,
    features_ref,
    params_ref,
    scaled_ref,
    sums_ref,
):
    frames, rows, cols, channels = features_ref.shape
    cells = rows * cols
    wide = 3 * channels
    mean = params_ref[0:frames]
    rstd = params_ref[frames : 2 * frames]
    gain = params_ref[2 * frames : 2 * frames + 1]
    bias = params_ref[2 * frames + 1 : 2 * frames + 2]
    is_last = lax.axis_index("tm") == lax.axis_size("tm") - 1
    for t in range(frames):
        acc = None
        for lag_t in range(3):
            for lag_h in range(3):
                f = t + far_ref.shape[0] - lag_t
                source = near_ref.at[f] if f < frames else far_ref.at[f - frames]
                window = source[2 - lag_h : 2 - lag_h + rows]
                taps = jnp.concatenate(
                    [weight_ref[lag_t, lag_h, 2 - e] for e in range(3)], axis=1
                )
                term = lax.dot_general(
                    window.reshape(cells, wide),
                    taps,
                    (((1,), (1,)), ((), ())),
                    preferred_element_type=jnp.float32,
                )
                acc = term if acc is None else acc + term
        later = t - (frames - future_ref.shape[0])
        if later >= 0:
            tail = future_ref[later].astype(jnp.float32).reshape(cells, channels)
            acc = acc + jnp.where(is_last, tail, jnp.zeros_like(tail))
        value = features_ref[t].astype(jnp.float32).reshape(cells, channels)
        centred = (value - mean[t : t + 1]) * rstd[t : t + 1]
        pre_act = centred * gain + bias
        sig = jax.nn.sigmoid(pre_act)
        scaled = acc * sig * (1.0 + pre_act * (1.0 - sig)) * gain
        scaled_ref[t] = scaled.reshape(rows, cols, channels)
        sums_ref[t : t + 1, :] = jnp.sum(scaled, axis=0, keepdims=True)
        sums_ref[frames + t : frames + t + 1, :] = jnp.sum(
            scaled * centred, axis=0, keepdims=True
        )


def final_kernel(groups, count, terms, *refs):
    parts, (scaled_ref, features_ref, grad_ref, params_ref, out_ref) = refs[:terms], refs[terms:]
    frames, _, _, channels = features_ref.shape
    mean = params_ref[0:frames]
    rstd = params_ref[frames : 2 * frames]
    total = parts[0][...]
    for part in parts[1:]:
        total = total + part[...]
    width = channels // groups
    means = exact_dot(total, group_matrix(channels, channels, width, width)) / count
    for t in range(frames):
        value = features_ref[t].astype(jnp.float32)
        centred = (value - mean[t : t + 1]) * rstd[t : t + 1]
        first = means[t : t + 1]
        second = means[frames + t : frames + t + 1]
        corrected = rstd[t : t + 1] * (scaled_ref[t] - first - centred * second)
        out_ref[t] = (grad_ref[t].astype(jnp.float32) + corrected).astype(jnp.bfloat16)


def call(kernel, out_shape, scratch=(), flops=0, moved=0, in_specs=None, out_specs=None):
    here = pl.BlockSpec(memory_space=pltpu.VMEM)

    def run(*args):
        return pl.pallas_call(
            kernel,
            out_shape=out_shape,
            in_specs=in_specs or [here] * len(args),
            out_specs=out_specs or jax.tree.map(lambda _: here, out_shape),
            scratch_shapes=list(scratch),
            compiler_params=pltpu.CompilerParams(vmem_limit_bytes=VMEM_BYTES),
            cost_estimate=pl.CostEstimate(flops=flops, bytes_accessed=moved, transcendentals=0),
        )(*args)

    return run


def extended(cells, sides, width):
    for axis, dim in sides:
        head = lax.slice_in_dim(cells, 0, width, axis=dim)
        tail = lax.slice_in_dim(cells, cells.shape[dim] - width, cells.shape[dim], axis=dim)
        cells = jnp.concatenate(
            [shifted(tail, axis, 1), cells, shifted(head, axis, -1)], axis=dim
        )
    return cells


def rims(grad_out, extra):
    frames, rows, cols, channels = grad_out.shape

    def piece(*shape):
        return jax.ShapeDtypeStruct((*shape, channels), grad_out.dtype)

    halo, row, col, corner, held = call(
        cut_kernel,
        (
            piece(extra, rows, cols),
            piece(frames, cols),
            piece(frames, rows),
            piece(frames),
            piece(frames, rows, cols),
        ),
    )(grad_out)
    halo = shifted(halo, "tm", -1)
    row = exchanged(row, "height", 1)
    corner = lax.ppermute(corner, ("height", "width"), [(i, 3 - i) for i in range(4)])
    col = exchanged(col, "width", 1)
    packed = call(pack_kernel, piece(extra, cols + rows + 1))(row, col, corner)
    tail = shifted(packed, "tm", -1)
    return (held, row, col, corner), (halo, tail)


def on_device(features, grad_out, mean_saved, rstd_saved, gain, bias, weight, future_cot):
    frames, rows, cols, channels = features.shape
    extra = weight.shape[0] - 1
    cells = rows * cols
    groups = mean_saved.shape[1]
    blocks = lax.axis_size("tm")
    taps = math.prod(weight.shape[:3])
    rows_out = taps * channels // blocks
    positions = cells * lax.axis_size("height") * lax.axis_size("width")
    grad_scale = 1.0 / math.sqrt(positions * frames * blocks)
    gain = gain.reshape(1, channels)
    bias = bias.reshape(1, channels)
    pair = paired()
    halves = in_halves(blocks, rows_out)
    f32 = jnp.float32

    if pair:
        near_sources, far_sources = rims(grad_out, extra)
    else:
        padded = extended(grad_out, (("height", 1), ("width", 2)), 1)
        sides = ((0, 0), (0, 0), (LEAD - 1, LEAD - 1), (0, 0))
        near_sources = (jnp.pad(padded, sides),)
        far_sources = (jnp.pad(shifted(padded[:extra], "tm", -1), sides),)

    inputs = tuple(
        pltpu.with_memory_space_constraint(value, pltpu.HBM)
        for value in (features, mean_saved, rstd_saved, gain, bias)
    )
    act, params = call(
        act_kernel,
        (
            jax.ShapeDtypeStruct((channels, frames * cells), jnp.bfloat16),
            jax.ShapeDtypeStruct((2 * frames + 2, channels), f32),
        ),
        scratch=(
            *[pltpu.VMEM(value.shape, value.dtype) for value in inputs],
            pltpu.SemaphoreType.DMA((len(inputs),)),
        ),
        in_specs=[pl.BlockSpec(memory_space=pltpu.HBM)] * len(inputs),
        flops=20 * frames * cells * channels,
        moved=4 * frames * cells * channels,
    )(*inputs)

    def window_shape(count):
        return jax.ShapeDtypeStruct((count, rows + 2, cols, 3 * channels), jnp.bfloat16)

    def stage_shape(count):
        return pltpu.VMEM((count, rows + 2, cols + 2 * LEAD, channels), f32)

    work = 2 * taps * channels * channels * frames * cells
    sum_shape = jax.ShapeDtypeStruct((taps * channels, channels), f32)
    near_window, near_sum = call(
        functools.partial(near_kernel, grad_scale, pair, extra),
        (window_shape(frames), sum_shape),
        scratch=(stage_shape(frames),),
        flops=3 * work // 4,
        moved=4 * 1024 * 1024,
    )(act, *near_sources)

    if halves:
        half_shape = jax.ShapeDtypeStruct((blocks, rows_out // 2, channels), f32)
        sum_shapes = (half_shape, half_shape)
    else:
        sum_shapes = (sum_shape,)
    far_window, *sums = call(
        functools.partial(far_kernel, rows_out, grad_scale, pair, halves, frames),
        (window_shape(extra), *sum_shapes),
        scratch=(stage_shape(extra), pltpu.VMEM((taps * channels, channels), f32)),
        flops=work // 4,
        moved=4 * 1024 * 1024,
    )(act, near_sum, *far_sources)

    if halves:
        weight_grad = reduced_share(*sums, rows_out)
    else:
        share = lax.psum_scatter(sums[0], "tm", scatter_dimension=0, tiled=True)
        weight_grad = lax.psum(share, ("height", "width"))

    scaled, local = call(
        conv_kernel,
        (
            jax.ShapeDtypeStruct((frames, rows, cols, channels), f32),
            jax.ShapeDtypeStruct((2 * frames, channels), f32),
        ),
        flops=work,
        moved=8 * 1024 * 1024,
    )(near_window, far_window, weight, future_cot, features, params)

    if pair:
        parts = [local]
        parts.append(exchanged(local, "width", 1))
        parts.append(exchanged(local, "height", 1))
        parts.append(
            lax.ppermute(local, ("height", "width"), [(i, 3 - i) for i in range(4)])
        )
    else:
        parts = [lax.psum(local, ("height", "width"))]
    input_cot = call(
        functools.partial(final_kernel, groups, positions * (channels // groups), len(parts)),
        jax.ShapeDtypeStruct(features.shape, jnp.bfloat16),
        flops=20 * frames * cells * channels,
        moved=10 * frames * cells * channels,
        out_specs=pl.BlockSpec(features.shape, lambda: (0, 0, 0, 0)),
    )(*parts, scaled, features, grad_out, params)
    return (input_cot, weight_grad)


def solution(mesh):
    placed = (
        P("tm", "height", "width", None),
        P("tm", "height", "width", None),
        P("tm", None),
        P("tm", None),
        P(),
        P(),
        P(),
        P(None, "height", "width", None),
    )
    return jax.shard_map(
        on_device,
        mesh=mesh,
        in_specs=placed,
        out_specs=(P("tm", "height", "width", None), P("tm", None)),
        check_vma=False,
    )
```

```python
import functools
import math

import jax
import jax.numpy as jnp
from jax import lax
from jax.experimental import pallas as pl
from jax.experimental.pallas import tpu as pltpu
from jax.sharding import PartitionSpec as P


LEAD = 8
VMEM_BYTES = 12 * 1024 * 1024


def exchanged(value, axis, distance):
    count = lax.axis_size(axis)
    return lax.ppermute(value, axis, [(i, i ^ distance) for i in range(count)])


def shifted(value, axis, steps):
    count = lax.axis_size(axis)
    initial, last = (max(0, -steps), min(count, count - steps))
    return lax.ppermute(value, axis, [(source, source + steps) for source in range(initial, last)])


def power_of_two(count):
    return count & (count - 1) == 0


def paired():
    return lax.axis_size("height") == 2 and lax.axis_size("width") == 2


def in_halves(blocks, rows):
    return paired() and power_of_two(blocks) and blocks >= 8 and rows % 16 == 0


def tm_side(distance):
    return (lax.axis_index("tm") // distance) % 2


def first_kernel(mine_ref, got_ref, low_near, low_far, high_near, high_far):
    half = mine_ref.shape[0] // 2
    near_side, next_side = tm_side(1), tm_side(2)

    def block(at):
        return mine_ref[at] + got_ref[at]

    for i in range(low_near.shape[0]):
        low_near[i] = block(2 * i + near_side)
        low_far[i] = block(2 * i + 1 - near_side).astype(low_far.dtype)
    for i in range(high_near.shape[0]):
        at = half + 4 * (i // 2) + i % 2
        high_near[i] = block(at + 2 * next_side)
        high_far[i] = block(at + 2 * (1 - next_side)).astype(high_far.dtype)


def second_kernel(low_ref, low_got_ref, high_ref, high_got_ref, *outs):
    low_near, low_far, high_near, high_far = outs

    def halve(value_ref, got_ref, near_ref, far_ref, side):
        for i in range(near_ref.shape[0]):
            at = 2 * i + side
            near_ref[i] = value_ref[at] + got_ref[at].astype(jnp.float32)
            at = 2 * i + 1 - side
            value = value_ref[at] + got_ref[at].astype(jnp.float32)
            far_ref[i] = value.astype(far_ref.dtype)

    halve(low_ref, low_got_ref, low_near, low_far, tm_side(2))
    halve(high_ref, high_got_ref, high_near, high_far, tm_side(1))


def split_kernel(distance, *refs):
    *parts, near_ref, far_ref = refs
    blocks = [
        (value_ref, got_ref, at)
        for value_ref, got_ref in zip(parts[::2], parts[1::2])
        for at in range(value_ref.shape[0])
    ]

    def block(i):
        value_ref, got_ref, at = blocks[i]
        return value_ref[at] + got_ref[at].astype(jnp.float32)

    for which in range(2):

        @pl.when(tm_side(distance) == which)
        def _():
            for i in range(near_ref.shape[0]):
                near_ref[i] = block(2 * i + which)
                far_ref[i] = block(2 * i + 1 - which).astype(far_ref.dtype)


def add_kernel(own_ref, got_ref, out_ref):
    out_ref[...] = own_ref[...] + got_ref[...].astype(jnp.float32)


def whole_kernel(own_ref, got_ref, beside_ref, out_ref):
    half = own_ref.shape[1]
    side = lax.axis_index("width")
    mine = pl.multiple_of(side * half, 8)
    other = pl.multiple_of((1 - side) * half, 8)
    out_ref[pl.ds(mine, half), :] = own_ref[0] + got_ref[0]
    out_ref[pl.ds(other, half), :] = beside_ref[0]


def reduced_share(mine, theirs, rows):
    blocks, half, channels = mine.shape
    f32, wire = jnp.float32, jnp.bfloat16

    def both(count):
        return tuple(jax.ShapeDtypeStruct((count, half, channels), kind) for kind in (f32, wire))

    got = exchanged(theirs, "width", 1)
    low, low_far, high, high_far = call(
        first_kernel, (*both(blocks // 4), *both(blocks // 4))
    )(mine, got)
    low_got = exchanged(low_far, "tm", 1)
    high_got = exchanged(high_far, "tm", 2)
    low, low_far, high, high_far = call(
        second_kernel, (*both(blocks // 8), *both(blocks // 8))
    )(low, low_got, high, high_got)
    low_got = exchanged(low_far, "tm", 2)
    high_got = exchanged(high_far, "tm", 1)
    parts = (low, low_got, high, high_got)
    distance = 4
    while distance < blocks:
        near, far = call(
            functools.partial(split_kernel, distance), both(blocks // distance // 2)
        )(*parts)
        parts = (near, exchanged(far, "tm", distance))
        distance *= 2
    share = both(1)[0]
    own = call(add_kernel, share)(*parts)
    got = exchanged(own, "height", 1)
    total = call(add_kernel, share)(own, got)
    beside = exchanged(total, "width", 1)
    return call(
        whole_kernel,
        jax.ShapeDtypeStruct((rows, channels), f32),
        out_specs=pl.BlockSpec((rows, channels), lambda: (0, 0)),
    )(own, got, beside)


def group_matrix(rows, cols, row_width, col_width):
    row = lax.broadcasted_iota(jnp.int32, (rows, cols), 0) // row_width
    col = lax.broadcasted_iota(jnp.int32, (rows, cols), 1) // col_width
    return (row == col).astype(jnp.float32)


def exact_dot(left, right):
    return lax.dot_general(
        left,
        right,
        (((1,), (0,)), ((), ())),
        precision=lax.Precision.HIGHEST,
        preferred_element_type=jnp.float32,
    )


def per_channel(value, channels):
    groups = value.shape[1]
    return exact_dot(value, group_matrix(groups, channels, 1, channels // groups))


def cut_kernel(*refs):
    sources, (halo_ref, row_ref, col_ref, corner_ref), held, sems = (
        refs[:6],
        refs[6:10],
        refs[10:-1],
        refs[-1],
    )
    extra = halo_ref.shape[0]
    pairs = [(sources[0].at[0:extra], halo_ref), *zip(sources, held)]
    copies = [
        pltpu.make_async_copy(source, target, sems.at[i])
        for i, (source, target) in enumerate(pairs)
    ]
    for copy in copies:
        copy.start()
    for copy in copies:
        copy.wait()
    grad_ref, features_ref = held[:2]
    frames, rows, cols, _ = grad_ref.shape
    row_at = (1 - lax.axis_index("height")) * (rows - 1)
    taken = [grad_ref.at[f] for f in range(frames)]
    taken += [features_ref.at[f] for f in range(frames - extra, frames)]

    def columns(at):
        corners = []
        for i, ref in enumerate(taken):
            col_ref[i] = ref[...].astype(jnp.float32)[:, at].astype(jnp.bfloat16)
            corners.append(ref[row_at].astype(jnp.float32)[at : at + 1])
        corner_ref[...] = jnp.concatenate(corners, axis=0).astype(jnp.bfloat16)

    for i, ref in enumerate(taken):
        row_ref[i] = ref[row_at]

    @pl.when(lax.axis_index("width") == 0)
    def _():
        columns(cols - 1)

    @pl.when(lax.axis_index("width") == 1)
    def _():
        columns(0)


def pack_kernel(row_ref, col_ref, corner_ref, tail_ref):
    cols, rows = row_ref.shape[1], col_ref.shape[1]
    for f in range(tail_ref.shape[0]):
        tail_ref[f, 0:cols] = row_ref[f]
        tail_ref[f, cols : cols + rows] = col_ref[f]
        tail_ref[f, cols + rows :] = corner_ref[f : f + 1]


def activation(value, params, frames, t):
    centred = (value - params[t : t + 1]) * params[frames + t : frames + t + 1]
    pre_act = centred * params[2 * frames : 2 * frames + 1]
    pre_act = pre_act + params[2 * frames + 1 : 2 * frames + 2]
    sig = jax.nn.sigmoid(pre_act)
    return centred, pre_act, sig


def act_kernel(
    features_ref, mean_ref, rstd_ref, gain_ref, bias_ref, act_ref, last_ref, params_ref
):
    frames, rows, cols, channels = features_ref.shape
    cells = rows * cols
    mean = per_channel(mean_ref[...], channels)
    rstd = per_channel(rstd_ref[...], channels)
    params = jnp.concatenate([mean, rstd, gain_ref[...], bias_ref[...]], axis=0)
    params_ref[...] = params
    for t in range(frames):
        value = features_ref[t].astype(jnp.float32).reshape(cells, channels)
        _, pre_act, sig = activation(value, params, frames, t)
        act = (pre_act * sig).astype(jnp.bfloat16)
        act_ref[:, t * cells : (t + 1) * cells] = act.T
        later = t - (frames - last_ref.shape[0])
        if later >= 0:
            last_ref[later] = act.reshape(rows, cols, channels)


def fill_pair(stage_ref, inner_ref, row_of, col_of, corner_of):
    total, rows, cols, channels = inner_ref.shape
    row_side = lax.axis_index("height")
    col_side = lax.axis_index("width")
    rim_row = (1 - row_side) * (rows + 1)
    for f in range(total):
        zeros = jnp.zeros((rows + 2, LEAD, channels), jnp.float32)
        stage_ref[f, :, 0:LEAD, :] = zeros
        stage_ref[f, :, LEAD + cols :, :] = zeros
        empty = jnp.zeros((cols, channels), jnp.float32)
        stage_ref[f, 0, LEAD : LEAD + cols, :] = empty
        stage_ref[f, rows + 1, LEAD : LEAD + cols, :] = empty
        stage_ref[f, 1 : rows + 1, LEAD : LEAD + cols, :] = inner_ref[f].astype(jnp.float32)
        stage_ref[f, rim_row, LEAD : LEAD + cols, :] = row_of(f).astype(jnp.float32)

    def fill_columns(at):
        for f in range(total):
            column = col_of(f).astype(jnp.float32)
            for r in range(rows):
                stage_ref[f, r + 1, at : at + 1, :] = column[r : r + 1]
            stage_ref[f, rim_row, at : at + 1, :] = corner_of(f).astype(jnp.float32)

    @pl.when(col_side == 1)
    def _():
        fill_columns(LEAD - 1)

    @pl.when(col_side == 0)
    def _():
        fill_columns(LEAD + cols)


def widen(stage_ref, window_ref):
    total, _, cols, wide = window_ref.shape
    channels = wide // 3

    def one(f, carry):
        for e in range(3):
            at = LEAD - 1 + e
            window_ref[f, :, :, e * channels : (e + 1) * channels] = stage_ref[
                f, :, at : at + cols, :
            ].astype(jnp.bfloat16)
        return carry

    lax.fori_loop(0, total, one, 0)


def tap_sums(act_ref, scale, pairs, window_of, shape, lag_t, add):
    rows, cols, channels = shape
    cells = rows * cols
    for lag_h in range(3):
        acc = None
        for t, f in pairs:
            window = window_of(f)[2 - lag_h : 2 - lag_h + rows]
            term = lax.dot_general(
                act_ref[:, t * cells : (t + 1) * cells],
                window.reshape(cells, window.shape[-1]),
                (((1,), (0,)), ((), ())),
                preferred_element_type=jnp.float32,
            )
            acc = term if acc is None else acc + term
        for lag_w in range(3):
            e = 2 - lag_w
            at = ((lag_t * 3 + lag_h) * 3 + lag_w) * channels
            if acc is None:
                value = jnp.zeros((channels, channels), jnp.float32)
            else:
                value = scale * acc[:, e * channels : (e + 1) * channels]
            add(at, value)


def near_kernel(scale, pair, extra, act_ref, *refs):
    sources, (window_ref, sum_ref, act_window_ref, stage_ref) = refs[:-4], refs[-4:]
    frames, rows_ext, cols, wide = window_ref.shape
    shape = (rows_ext - 2, cols, wide // 3)
    if pair:
        grad_ref, row_ref, col_ref, corner_ref, last_ref, params_ref = sources
        params = params_ref[...]

        def rim_act(value, f):
            value = value.astype(jnp.float32)
            _, pre_act, sig = activation(value, params, frames, frames - extra + f)
            return (pre_act * sig).astype(jnp.bfloat16)

        fill_pair(
            stage_ref,
            grad_ref,
            lambda f: row_ref[f],
            lambda f: col_ref[f],
            lambda f: corner_ref[f : f + 1],
        )
        widen(stage_ref, window_ref)
        fill_pair(
            stage_ref,
            last_ref,
            lambda f: rim_act(row_ref[frames + f], f),
            lambda f: rim_act(col_ref[frames + f], f),
            lambda f: rim_act(corner_ref[frames + f : frames + f + 1], f),
        )
        widen(stage_ref, act_window_ref)
    else:
        stage_ref[...] = sources[0][...].astype(jnp.float32)
        widen(stage_ref, window_ref)
        stage_ref[:extra] = sources[1][...].astype(jnp.float32)
        widen(stage_ref, act_window_ref)

    def put(at, value):
        sum_ref[at : at + value.shape[0], :] = value

    for lag_t in range(extra + 1):
        ahead = extra - lag_t
        pairs = [(t, t + ahead) for t in range(frames) if t + ahead < frames]
        tap_sums(act_ref, scale, pairs, lambda f: window_ref.at[f], shape, lag_t, put)


def far_kernel(rows_out, scale, halves, frames, act_window_ref, near_sum_ref, halo_ref, *refs):
    outs, sum_ref = refs[:-1], refs[-1]
    extra, rows, cols, channels = halo_ref.shape
    cells = rows * cols
    flipped = [halo_ref[f].reshape(cells, channels).T for f in range(extra)]
    for lag_t in range(extra):
        ahead = extra - lag_t
        pairs = [(t, t + ahead - frames) for t in range(frames) if t + ahead >= frames]
        for lag_h in range(3):
            acc = None
            for t, f in pairs:
                window = act_window_ref[t - (frames - extra), lag_h : lag_h + rows]
                term = lax.dot_general(
                    flipped[f],
                    window.reshape(cells, 3 * channels),
                    (((1,), (0,)), ((), ())),
                    preferred_element_type=jnp.float32,
                )
                acc = term if acc is None else acc + term
            for lag_w in range(3):
                at = ((lag_t * 3 + lag_h) * 3 + lag_w) * channels
                value = scale * acc[:, lag_w * channels : (lag_w + 1) * channels].T
                sum_ref[at : at + channels, :] = near_sum_ref[at : at + channels, :] + value
    done = extra * 9 * channels
    sum_ref[done:, :] = near_sum_ref[done:, :]
    if not halves:
        outs[0][...] = sum_ref[...]
        return
    mine_ref, theirs_ref = outs
    col_side = lax.axis_index("width")
    half = rows_out // 2

    def place(low_ref, high_ref):
        for block in range(mine_ref.shape[0]):
            at = block * rows_out
            low_ref[block] = sum_ref[at : at + half, :]
            high_ref[block] = sum_ref[at + half : at + rows_out, :]

    @pl.when(col_side == 0)
    def _():
        place(mine_ref, theirs_ref)

    @pl.when(col_side == 1)
    def _():
        place(theirs_ref, mine_ref)


def conv_frames(window_of, weight_ref, future_ref, features_ref, params, span, scaled_ref, put):
    frames, rows, cols, channels = features_ref.shape
    cells = rows * cols
    extra = weight_ref.shape[0] - 1
    gain = params[2 * frames : 2 * frames + 1]
    is_last = lax.axis_index("tm") == lax.axis_size("tm") - 1
    for t in span:
        acc = None
        for lag_t in range(extra + 1):
            for lag_h in range(3):
                window = window_of(t + extra - lag_t)[2 - lag_h : 2 - lag_h + rows]
                taps = jnp.concatenate(
                    [weight_ref[lag_t, lag_h, 2 - e] for e in range(3)], axis=1
                )
                term = lax.dot_general(
                    window.reshape(cells, 3 * channels),
                    taps,
                    (((1,), (1,)), ((), ())),
                    preferred_element_type=jnp.float32,
                )
                acc = term if acc is None else acc + term
        later = t - (frames - extra)
        if later >= 0:
            tail = future_ref[later].astype(jnp.float32).reshape(cells, channels)
            acc = acc + jnp.where(is_last, tail, jnp.zeros_like(tail))
        value = features_ref[t].astype(jnp.float32).reshape(cells, channels)
        centred, pre_act, sig = activation(value, params, frames, t)
        scaled = acc * sig * (1.0 + pre_act * (1.0 - sig)) * gain
        scaled_ref[t - span[0]] = scaled.reshape(rows, cols, channels)
        put(t, jnp.sum(scaled, axis=0, keepdims=True))
        put(frames + t, jnp.sum(scaled * centred, axis=0, keepdims=True))


def early_kernel(near_ref, weight_ref, features_ref, params_ref, scaled_ref, sums_ref):
    sums_ref[...] = jnp.zeros_like(sums_ref)

    def put(at, value):
        sums_ref[at : at + 1, :] = value

    conv_frames(
        lambda f: near_ref.at[f],
        weight_ref,
        None,
        features_ref,
        params_ref[...],
        range(scaled_ref.shape[0]),
        scaled_ref,
        put,
    )


def late_kernel(pair, early, *refs):
    count = 2 if pair else 1
    sources = refs[:count]
    near_ref, weight_ref, future_ref, features_ref, params_ref = refs[count : count + 5]
    before, (scaled_ref, sums_ref, window_ref, stage_ref) = refs[count + 5 : -4], refs[-4:]
    frames, rows, cols, _ = features_ref.shape
    if pair:
        halo_ref, tail_ref = sources
        fill_pair(
            stage_ref,
            halo_ref,
            lambda f: tail_ref[f, 0:cols],
            lambda f: tail_ref[f, cols : cols + rows],
            lambda f: tail_ref[f, cols + rows : cols + rows + 1],
        )
    else:
        stage_ref[...] = sources[0][...].astype(jnp.float32)
    widen(stage_ref, window_ref)
    if before:
        sums_ref[...] = before[0][...]

    def put(at, value):
        sums_ref[at : at + 1, :] = value

    conv_frames(
        lambda f: near_ref.at[f] if f < frames else window_ref.at[f - frames],
        weight_ref,
        future_ref,
        features_ref,
        params_ref[...],
        range(early, frames),
        scaled_ref,
        put,
    )


def final_kernel(groups, count, terms, *refs):
    parts, scaled_refs, (features_ref, grad_ref, params_ref, out_ref) = (
        refs[:terms],
        refs[terms:-4],
        refs[-4:],
    )
    scaled = [ref.at[t] for ref in scaled_refs for t in range(ref.shape[0])]
    frames, _, _, channels = features_ref.shape
    mean = params_ref[0:frames]
    rstd = params_ref[frames : 2 * frames]
    total = parts[0][...]
    for part in parts[1:]:
        total = total + part[...]
    width = channels // groups
    means = exact_dot(total, group_matrix(channels, channels, width, width)) / count
    for t in range(frames):
        value = features_ref[t].astype(jnp.float32)
        centred = (value - mean[t : t + 1]) * rstd[t : t + 1]
        first = means[t : t + 1]
        second = means[frames + t : frames + t + 1]
        corrected = rstd[t : t + 1] * (scaled[t][...] - first - centred * second)
        out_ref[t] = (grad_ref[t].astype(jnp.float32) + corrected).astype(jnp.bfloat16)


def call(kernel, out_shape, scratch=(), flops=0, moved=0, in_specs=None, out_specs=None):
    here = pl.BlockSpec(memory_space=pltpu.VMEM)

    def run(*args):
        return pl.pallas_call(
            kernel,
            out_shape=out_shape,
            in_specs=in_specs or [here] * len(args),
            out_specs=out_specs or jax.tree.map(lambda _: here, out_shape),
            scratch_shapes=list(scratch),
            compiler_params=pltpu.CompilerParams(vmem_limit_bytes=VMEM_BYTES),
            cost_estimate=pl.CostEstimate(flops=flops, bytes_accessed=moved, transcendentals=0),
        )(*args)

    return run


def extended(cells, sides, width):
    for axis, dim in sides:
        head = lax.slice_in_dim(cells, 0, width, axis=dim)
        tail = lax.slice_in_dim(cells, cells.shape[dim] - width, cells.shape[dim], axis=dim)
        cells = jnp.concatenate(
            [shifted(tail, axis, 1), cells, shifted(head, axis, -1)], axis=dim
        )
    return cells


def rims(inputs, extra):
    frames, rows, cols, channels = inputs[0].shape

    def piece(*shape):
        return jax.ShapeDtypeStruct((*shape, channels), inputs[0].dtype)

    halo, row, col, corner, *held = call(
        cut_kernel,
        (
            piece(extra, rows, cols),
            piece(frames + extra, cols),
            piece(frames + extra, rows),
            piece(frames + extra),
            *[jax.ShapeDtypeStruct(value.shape, value.dtype) for value in inputs],
        ),
        scratch=(pltpu.SemaphoreType.DMA((len(inputs) + 1,)),),
        in_specs=[pl.BlockSpec(memory_space=pltpu.HBM)] * len(inputs),
    )(*[pltpu.with_memory_space_constraint(value, pltpu.HBM) for value in inputs])
    halo = shifted(halo, "tm", -1)
    row = exchanged(row, "height", 1)
    corner = lax.ppermute(corner, ("height", "width"), [(i, 3 - i) for i in range(4)])
    col = exchanged(col, "width", 1)
    packed = call(pack_kernel, piece(extra, cols + rows + 1))(row, col, corner)
    tail = shifted(packed, "tm", -1)
    return held, (row, col, corner), (halo, tail)


def on_device(features, grad_out, mean_saved, rstd_saved, gain, bias, weight, future_cot):
    frames, rows, cols, channels = features.shape
    extra = weight.shape[0] - 1
    cells = rows * cols
    groups = mean_saved.shape[1]
    blocks = lax.axis_size("tm")
    taps = math.prod(weight.shape[:3])
    rows_out = taps * channels // blocks
    positions = cells * lax.axis_size("height") * lax.axis_size("width")
    grad_scale = 1.0 / math.sqrt(positions * frames * blocks)
    gain = gain.reshape(1, channels)
    bias = bias.reshape(1, channels)
    pair = paired()
    halves = in_halves(blocks, rows_out)
    f32, bf16 = jnp.float32, jnp.bfloat16
    work = 2 * taps * channels * channels * frames * cells
    early = frames - extra

    def shape(*dims, kind=f32):
        return jax.ShapeDtypeStruct((*dims, channels), kind)

    def window_shape(count):
        return jax.ShapeDtypeStruct((count, rows + 2, cols, 3 * channels), bf16)

    def stage_shape(count):
        return pltpu.VMEM((count, rows + 2, cols + 2 * LEAD, channels), f32)

    if pair:
        held, near_rims, (halo, tail) = rims(
            (grad_out, features, mean_saved, rstd_saved, gain, bias), extra
        )
        grad_out, features, mean_saved, rstd_saved, gain, bias = held
        late_sources = (halo, tail)

    act, last, params = call(
        act_kernel,
        (
            jax.ShapeDtypeStruct((channels, frames * cells), bf16),
            shape(extra, rows, cols, kind=bf16),
            shape(2 * frames + 2),
        ),
        flops=20 * frames * cells * channels,
        moved=4 * frames * cells * channels,
    )(features, mean_saved, rstd_saved, gain, bias)

    if pair:
        near_sources = (grad_out, *near_rims, last, params)
    else:
        axes = (("height", 1), ("width", 2))
        sides = ((0, 0), (0, 0), (LEAD - 1, LEAD - 1), (0, 0))
        padded = extended(grad_out, axes, 1)
        near_sources = (jnp.pad(padded, sides), jnp.pad(extended(last, axes, 1), sides))
        halo = shifted(grad_out[:extra], "tm", -1)
        late_sources = (jnp.pad(shifted(padded[:extra], "tm", -1), sides),)

    near_window, near_sum, act_window = call(
        functools.partial(near_kernel, grad_scale, pair, extra),
        (window_shape(frames), shape(taps * channels), window_shape(extra)),
        scratch=(stage_shape(frames),),
        flops=3 * work // 4,
        moved=4 * 1024 * 1024,
    )(act, *near_sources)

    if halves:
        sum_shapes = (shape(blocks, rows_out // 2), shape(blocks, rows_out // 2))
    else:
        sum_shapes = (shape(taps * channels),)
    sums = call(
        functools.partial(far_kernel, rows_out, grad_scale, halves, frames),
        sum_shapes,
        scratch=(pltpu.VMEM((taps * channels, channels), f32),),
        flops=work // 4,
        moved=4 * 1024 * 1024,
    )(act_window, near_sum, halo)

    if halves:
        weight_grad = reduced_share(*sums, rows_out)
    else:
        share = lax.psum_scatter(sums[0], "tm", scatter_dimension=0, tiled=True)
        weight_grad = lax.psum(share, ("height", "width"))

    scaled, before = [], []
    if early:
        value, local = call(
            early_kernel,
            (shape(early, rows, cols), shape(2 * frames)),
            flops=work * early // frames,
            moved=4 * 1024 * 1024,
        )(near_window, weight, features, params)
        scaled.append(value)
        before.append(local)
    value, local = call(
        functools.partial(late_kernel, pair, early),
        (shape(extra, rows, cols), shape(2 * frames)),
        scratch=(
            pltpu.VMEM(window_shape(extra).shape, bf16),
            stage_shape(extra),
        ),
        flops=work * extra // frames,
        moved=4 * 1024 * 1024,
    )(*late_sources, near_window, weight, future_cot, features, params, *before)
    scaled.append(value)

    if pair:
        parts = [local]
        parts.append(exchanged(local, "width", 1))
        parts.append(exchanged(local, "height", 1))
        parts.append(
            lax.ppermute(local, ("height", "width"), [(i, 3 - i) for i in range(4)])
        )
    else:
        parts = [lax.psum(local, ("height", "width"))]
    input_cot = call(
        functools.partial(final_kernel, groups, positions * (channels // groups), len(parts)),
        shape(frames, rows, cols, kind=bf16),
        flops=20 * frames * cells * channels,
        moved=10 * frames * cells * channels,
        out_specs=pl.BlockSpec(features.shape, lambda: (0, 0, 0, 0)),
    )(*parts, *scaled, features, grad_out, params)
    return (input_cot, weight_grad)


def solution(mesh):
    placed = (
        P("tm", "height", "width", None),
        P("tm", "height", "width", None),
        P("tm", None),
        P("tm", None),
        P(),
        P(),
        P(),
        P(None, "height", "width", None),
    )
    return jax.shard_map(
        on_device,
        mesh=mesh,
        in_specs=placed,
        out_specs=(P("tm", "height", "width", None), P("tm", None)),
        check_vma=False,
    )
```

```python
import functools
import math

import jax
import jax.numpy as jnp
from jax import lax
from jax.experimental import pallas as pl
from jax.experimental.pallas import tpu as pltpu
from jax.sharding import PartitionSpec as P


LEAD = 8
VMEM_BYTES = 12 * 1024 * 1024


def exchanged(value, axis, distance):
    count = lax.axis_size(axis)
    return lax.ppermute(value, axis, [(i, i ^ distance) for i in range(count)])


def shifted(value, axis, steps):
    count = lax.axis_size(axis)
    initial, last = (max(0, -steps), min(count, count - steps))
    return lax.ppermute(value, axis, [(source, source + steps) for source in range(initial, last)])


def power_of_two(count):
    return count & (count - 1) == 0


def paired():
    return lax.axis_size("height") == 2 and lax.axis_size("width") == 2


def in_halves(blocks, rows):
    return paired() and power_of_two(blocks) and blocks >= 8 and rows % 16 == 0


def tm_side(distance):
    return (lax.axis_index("tm") // distance) % 2


def first_kernel(mine_ref, got_ref, low_near, low_far, high_near, high_far):
    half = mine_ref.shape[0] // 2
    near_side, next_side = tm_side(1), tm_side(2)

    def block(at):
        return mine_ref[at] + got_ref[at].astype(jnp.float32)

    for i in range(low_near.shape[0]):
        low_near[i] = block(2 * i + near_side)
        low_far[i] = block(2 * i + 1 - near_side).astype(low_far.dtype)
    for i in range(high_near.shape[0]):
        at = half + 4 * (i // 2) + i % 2
        high_near[i] = block(at + 2 * next_side)
        high_far[i] = block(at + 2 * (1 - next_side)).astype(high_far.dtype)


def second_kernel(low_ref, low_got_ref, high_ref, high_got_ref, *outs):
    low_near, low_far, high_near, high_far = outs

    def halve(value_ref, got_ref, near_ref, far_ref, side):
        for i in range(near_ref.shape[0]):
            at = 2 * i + side
            near_ref[i] = value_ref[at] + got_ref[at].astype(jnp.float32)
            at = 2 * i + 1 - side
            value = value_ref[at] + got_ref[at].astype(jnp.float32)
            far_ref[i] = value.astype(far_ref.dtype)

    halve(low_ref, low_got_ref, low_near, low_far, tm_side(2))
    halve(high_ref, high_got_ref, high_near, high_far, tm_side(1))


def split_kernel(distance, *refs):
    *parts, near_ref, far_ref = refs
    blocks = [
        (value_ref, got_ref, at)
        for value_ref, got_ref in zip(parts[::2], parts[1::2])
        for at in range(value_ref.shape[0])
    ]

    def block(i):
        value_ref, got_ref, at = blocks[i]
        return value_ref[at] + got_ref[at].astype(jnp.float32)

    for which in range(2):

        @pl.when(tm_side(distance) == which)
        def _():
            for i in range(near_ref.shape[0]):
                near_ref[i] = block(2 * i + which)
                far_ref[i] = block(2 * i + 1 - which).astype(far_ref.dtype)


def total_kernel(own_ref, got_ref, below_ref, below_got_ref, out_ref):
    mine = own_ref[...] + got_ref[...].astype(jnp.float32)
    out_ref[...] = mine + (below_ref[...] + below_got_ref[...].astype(jnp.float32))


def whole_kernel(own_ref, beside_ref, out_ref):
    half = own_ref.shape[1]
    side = lax.axis_index("width")
    out_ref[pl.ds(pl.multiple_of(side * half, 8), half), :] = own_ref[0]
    out_ref[pl.ds(pl.multiple_of((1 - side) * half, 8), half), :] = beside_ref[0]


def reduced_share(mine, theirs, rows):
    blocks, half, channels = mine.shape
    f32, wire = jnp.float32, jnp.bfloat16

    def both(count):
        return tuple(jax.ShapeDtypeStruct((count, half, channels), kind) for kind in (f32, wire))

    got = exchanged(theirs, "width", 1)
    low, low_far, high, high_far = call(
        first_kernel, (*both(blocks // 4), *both(blocks // 4))
    )(mine, got)
    low_got = exchanged(low_far, "tm", 1)
    high_got = exchanged(high_far, "tm", 2)
    low, low_far, high, high_far = call(
        second_kernel, (*both(blocks // 8), *both(blocks // 8))
    )(low, low_got, high, high_got)
    low_got = exchanged(low_far, "tm", 2)
    high_got = exchanged(high_far, "tm", 1)
    parts = (low, low_got, high, high_got)
    distance = 4
    while distance < blocks:
        near, far = call(
            functools.partial(split_kernel, distance), both(blocks // distance // 2)
        )(*parts)
        parts = (near, exchanged(far, "tm", distance))
        distance *= 2
    own, got = parts
    below = exchanged(own, "height", 1)
    below_got = exchanged(got, "height", 1)
    total = call(total_kernel, both(1)[0])(own, got, below, below_got)
    beside = exchanged(total, "width", 1)
    return call(
        whole_kernel,
        jax.ShapeDtypeStruct((rows, channels), f32),
        out_specs=pl.BlockSpec((rows, channels), lambda: (0, 0)),
    )(total, beside)


def group_matrix(rows, cols, row_width, col_width):
    row = lax.broadcasted_iota(jnp.int32, (rows, cols), 0) // row_width
    col = lax.broadcasted_iota(jnp.int32, (rows, cols), 1) // col_width
    return (row == col).astype(jnp.float32)


def exact_dot(left, right):
    return lax.dot_general(
        left,
        right,
        (((1,), (0,)), ((), ())),
        precision=lax.Precision.HIGHEST,
        preferred_element_type=jnp.float32,
    )


def per_channel(value, channels):
    groups = value.shape[1]
    return exact_dot(value, group_matrix(groups, channels, 1, channels // groups))


def cut_kernel(*refs):
    sources, (halo_ref, row_ref, col_ref, corner_ref), held, sems = (
        refs[:6],
        refs[6:10],
        refs[10:-1],
        refs[-1],
    )
    extra = halo_ref.shape[0]
    pairs = [(sources[0].at[0:extra], halo_ref), *zip(sources, held)]
    copies = [
        pltpu.make_async_copy(source, target, sems.at[i])
        for i, (source, target) in enumerate(pairs)
    ]
    for copy in copies:
        copy.start()
    for copy in copies:
        copy.wait()
    grad_ref, features_ref = held[:2]
    frames, rows, cols, _ = grad_ref.shape
    row_at = (1 - lax.axis_index("height")) * (rows - 1)
    taken = [grad_ref.at[f] for f in range(frames)]
    taken += [features_ref.at[f] for f in range(frames - extra, frames)]

    def columns(at):
        corners = []
        for i, ref in enumerate(taken):
            col_ref[i] = ref[...].astype(jnp.float32)[:, at].astype(jnp.bfloat16)
            corners.append(ref[row_at].astype(jnp.float32)[at : at + 1])
        corner_ref[...] = jnp.concatenate(corners, axis=0).astype(jnp.bfloat16)

    for i, ref in enumerate(taken):
        row_ref[i] = ref[row_at]

    @pl.when(lax.axis_index("width") == 0)
    def _():
        columns(cols - 1)

    @pl.when(lax.axis_index("width") == 1)
    def _():
        columns(0)


def pack_kernel(row_ref, col_ref, corner_ref, tail_ref):
    cols, rows = row_ref.shape[1], col_ref.shape[1]
    for f in range(tail_ref.shape[0]):
        tail_ref[f, 0:cols] = row_ref[f]
        tail_ref[f, cols : cols + rows] = col_ref[f]
        tail_ref[f, cols + rows :] = corner_ref[f : f + 1]


def activation(value, params, frames, t):
    centred = (value - params[t : t + 1]) * params[frames + t : frames + t + 1]
    pre_act = centred * params[2 * frames : 2 * frames + 1]
    pre_act = pre_act + params[2 * frames + 1 : 2 * frames + 2]
    sig = jax.nn.sigmoid(pre_act)
    return centred, pre_act, sig


def act_kernel(
    features_ref, mean_ref, rstd_ref, gain_ref, bias_ref, act_ref, last_ref, params_ref
):
    frames, rows, cols, channels = features_ref.shape
    cells = rows * cols
    mean = per_channel(mean_ref[...], channels)
    rstd = per_channel(rstd_ref[...], channels)
    params = jnp.concatenate([mean, rstd, gain_ref[...], bias_ref[...]], axis=0)
    params_ref[...] = params
    for t in range(frames):
        value = features_ref[t].astype(jnp.float32).reshape(cells, channels)
        _, pre_act, sig = activation(value, params, frames, t)
        act = (pre_act * sig).astype(jnp.bfloat16)
        act_ref[:, t * cells : (t + 1) * cells] = act.T
        later = t - (frames - last_ref.shape[0])
        if later >= 0:
            last_ref[later] = act.reshape(rows, cols, channels)


def fill_pair(stage_ref, inner_ref, row_of, col_of, corner_of):
    total, rows, cols, channels = inner_ref.shape
    row_side = lax.axis_index("height")
    col_side = lax.axis_index("width")
    rim_row = (1 - row_side) * (rows + 1)
    for f in range(total):
        zeros = jnp.zeros((rows + 2, LEAD, channels), jnp.float32)
        stage_ref[f, :, 0:LEAD, :] = zeros
        stage_ref[f, :, LEAD + cols :, :] = zeros
        empty = jnp.zeros((cols, channels), jnp.float32)
        stage_ref[f, 0, LEAD : LEAD + cols, :] = empty
        stage_ref[f, rows + 1, LEAD : LEAD + cols, :] = empty
        stage_ref[f, 1 : rows + 1, LEAD : LEAD + cols, :] = inner_ref[f].astype(jnp.float32)
        stage_ref[f, rim_row, LEAD : LEAD + cols, :] = row_of(f).astype(jnp.float32)

    def fill_columns(at):
        for f in range(total):
            column = col_of(f).astype(jnp.float32)
            for r in range(rows):
                stage_ref[f, r + 1, at : at + 1, :] = column[r : r + 1]
            stage_ref[f, rim_row, at : at + 1, :] = corner_of(f).astype(jnp.float32)

    @pl.when(col_side == 1)
    def _():
        fill_columns(LEAD - 1)

    @pl.when(col_side == 0)
    def _():
        fill_columns(LEAD + cols)


def widen(stage_ref, window_ref):
    total, _, cols, wide = window_ref.shape
    channels = wide // 3

    def one(f, carry):
        for e in range(3):
            at = LEAD - 1 + e
            window_ref[f, :, :, e * channels : (e + 1) * channels] = stage_ref[
                f, :, at : at + cols, :
            ].astype(jnp.bfloat16)
        return carry

    lax.fori_loop(0, total, one, 0)


def tap_sums(act_ref, scale, pairs, window_of, shape, lag_t, add):
    rows, cols, channels = shape
    cells = rows * cols
    for lag_h in range(3):
        acc = None
        for t, f in pairs:
            window = window_of(f)[2 - lag_h : 2 - lag_h + rows]
            term = lax.dot_general(
                act_ref[:, t * cells : (t + 1) * cells],
                window.reshape(cells, window.shape[-1]),
                (((1,), (0,)), ((), ())),
                preferred_element_type=jnp.float32,
            )
            acc = term if acc is None else acc + term
        for lag_w in range(3):
            e = 2 - lag_w
            at = ((lag_t * 3 + lag_h) * 3 + lag_w) * channels
            if acc is None:
                value = jnp.zeros((channels, channels), jnp.float32)
            else:
                value = scale * acc[:, e * channels : (e + 1) * channels]
            add(at, value)


def near_kernel(scale, pair, extra, act_ref, *refs):
    sources, (window_ref, sum_ref, act_window_ref, stage_ref) = refs[:-4], refs[-4:]
    frames, rows_ext, cols, wide = window_ref.shape
    shape = (rows_ext - 2, cols, wide // 3)
    if pair:
        grad_ref, row_ref, col_ref, corner_ref, last_ref, params_ref = sources
        params = params_ref[...]

        def rim_act(value, f):
            value = value.astype(jnp.float32)
            _, pre_act, sig = activation(value, params, frames, frames - extra + f)
            return (pre_act * sig).astype(jnp.bfloat16)

        fill_pair(
            stage_ref,
            grad_ref,
            lambda f: row_ref[f],
            lambda f: col_ref[f],
            lambda f: corner_ref[f : f + 1],
        )
        widen(stage_ref, window_ref)
        fill_pair(
            stage_ref,
            last_ref,
            lambda f: rim_act(row_ref[frames + f], f),
            lambda f: rim_act(col_ref[frames + f], f),
            lambda f: rim_act(corner_ref[frames + f : frames + f + 1], f),
        )
        widen(stage_ref, act_window_ref)
    else:
        stage_ref[...] = sources[0][...].astype(jnp.float32)
        widen(stage_ref, window_ref)
        stage_ref[:extra] = sources[1][...].astype(jnp.float32)
        widen(stage_ref, act_window_ref)

    def put(at, value):
        sum_ref[at : at + value.shape[0], :] = value

    for lag_t in range(extra + 1):
        ahead = extra - lag_t
        pairs = [(t, t + ahead) for t in range(frames) if t + ahead < frames]
        tap_sums(act_ref, scale, pairs, lambda f: window_ref.at[f], shape, lag_t, put)


def far_kernel(rows_out, scale, halves, frames, act_window_ref, near_sum_ref, halo_ref, *refs):
    outs, sum_ref = refs[:-1], refs[-1]
    extra, rows, cols, channels = halo_ref.shape
    cells = rows * cols
    flipped = [halo_ref[f].reshape(cells, channels).T for f in range(extra)]
    for lag_t in range(extra):
        ahead = extra - lag_t
        pairs = [(t, t + ahead - frames) for t in range(frames) if t + ahead >= frames]
        for lag_h in range(3):
            acc = None
            for t, f in pairs:
                window = act_window_ref[t - (frames - extra), lag_h : lag_h + rows]
                term = lax.dot_general(
                    flipped[f],
                    window.reshape(cells, 3 * channels),
                    (((1,), (0,)), ((), ())),
                    preferred_element_type=jnp.float32,
                )
                acc = term if acc is None else acc + term
            for lag_w in range(3):
                at = ((lag_t * 3 + lag_h) * 3 + lag_w) * channels
                value = scale * acc[:, lag_w * channels : (lag_w + 1) * channels].T
                sum_ref[at : at + channels, :] = near_sum_ref[at : at + channels, :] + value
    done = extra * 9 * channels
    sum_ref[done:, :] = near_sum_ref[done:, :]
    if not halves:
        outs[0][...] = sum_ref[...]
        return
    mine_ref, theirs_ref = outs
    col_side = lax.axis_index("width")
    half = rows_out // 2

    def place(low_ref, high_ref):
        for block in range(mine_ref.shape[0]):
            at = block * rows_out
            low_ref[block] = sum_ref[at : at + half, :].astype(low_ref.dtype)
            high_ref[block] = sum_ref[at + half : at + rows_out, :].astype(high_ref.dtype)

    @pl.when(col_side == 0)
    def _():
        place(mine_ref, theirs_ref)

    @pl.when(col_side == 1)
    def _():
        place(theirs_ref, mine_ref)


def conv_frames(window_of, weight_ref, future_ref, features_ref, params, span, scaled_ref, put):
    frames, rows, cols, channels = features_ref.shape
    cells = rows * cols
    extra = weight_ref.shape[0] - 1
    gain = params[2 * frames : 2 * frames + 1]
    is_last = lax.axis_index("tm") == lax.axis_size("tm") - 1
    for t in span:
        acc = None
        for lag_t in range(extra + 1):
            for lag_h in range(3):
                window = window_of(t + extra - lag_t)[2 - lag_h : 2 - lag_h + rows]
                taps = jnp.concatenate(
                    [weight_ref[lag_t, lag_h, 2 - e] for e in range(3)], axis=1
                )
                term = lax.dot_general(
                    window.reshape(cells, 3 * channels),
                    taps,
                    (((1,), (1,)), ((), ())),
                    preferred_element_type=jnp.float32,
                )
                acc = term if acc is None else acc + term
        later = t - (frames - extra)
        if later >= 0:
            tail = future_ref[later].astype(jnp.float32).reshape(cells, channels)
            acc = acc + jnp.where(is_last, tail, jnp.zeros_like(tail))
        value = features_ref[t].astype(jnp.float32).reshape(cells, channels)
        centred, pre_act, sig = activation(value, params, frames, t)
        scaled = acc * sig * (1.0 + pre_act * (1.0 - sig)) * gain
        scaled_ref[t - span[0]] = scaled.reshape(rows, cols, channels)
        put(t, jnp.sum(scaled, axis=0, keepdims=True))
        put(frames + t, jnp.sum(scaled * centred, axis=0, keepdims=True))


def early_kernel(near_ref, weight_ref, features_ref, params_ref, scaled_ref, sums_ref):
    sums_ref[...] = jnp.zeros_like(sums_ref)

    def put(at, value):
        sums_ref[at : at + 1, :] = value

    conv_frames(
        lambda f: near_ref.at[f],
        weight_ref,
        None,
        features_ref,
        params_ref[...],
        range(scaled_ref.shape[0]),
        scaled_ref,
        put,
    )


def late_kernel(pair, early, *refs):
    count = 2 if pair else 1
    sources = refs[:count]
    near_ref, weight_ref, future_ref, features_ref, params_ref = refs[count : count + 5]
    before, (scaled_ref, sums_ref, window_ref, stage_ref) = refs[count + 5 : -4], refs[-4:]
    frames, rows, cols, _ = features_ref.shape
    if pair:
        halo_ref, tail_ref = sources
        fill_pair(
            stage_ref,
            halo_ref,
            lambda f: tail_ref[f, 0:cols],
            lambda f: tail_ref[f, cols : cols + rows],
            lambda f: tail_ref[f, cols + rows : cols + rows + 1],
        )
    else:
        stage_ref[...] = sources[0][...].astype(jnp.float32)
    widen(stage_ref, window_ref)
    if before:
        sums_ref[...] = before[0][...]

    def put(at, value):
        sums_ref[at : at + 1, :] = value

    conv_frames(
        lambda f: near_ref.at[f] if f < frames else window_ref.at[f - frames],
        weight_ref,
        future_ref,
        features_ref,
        params_ref[...],
        range(early, frames),
        scaled_ref,
        put,
    )


def final_kernel(groups, count, terms, *refs):
    parts, scaled_refs, (features_ref, grad_ref, params_ref, out_ref) = (
        refs[:terms],
        refs[terms:-4],
        refs[-4:],
    )
    scaled = [ref.at[t] for ref in scaled_refs for t in range(ref.shape[0])]
    frames, _, _, channels = features_ref.shape
    mean = params_ref[0:frames]
    rstd = params_ref[frames : 2 * frames]
    total = parts[0][...]
    for part in parts[1:]:
        total = total + part[...]
    width = channels // groups
    means = exact_dot(total, group_matrix(channels, channels, width, width)) / count
    for t in range(frames):
        value = features_ref[t].astype(jnp.float32)
        centred = (value - mean[t : t + 1]) * rstd[t : t + 1]
        first = means[t : t + 1]
        second = means[frames + t : frames + t + 1]
        corrected = rstd[t : t + 1] * (scaled[t][...] - first - centred * second)
        out_ref[t] = (grad_ref[t].astype(jnp.float32) + corrected).astype(jnp.bfloat16)


def call(kernel, out_shape, scratch=(), flops=0, moved=0, in_specs=None, out_specs=None):
    here = pl.BlockSpec(memory_space=pltpu.VMEM)

    def run(*args):
        return pl.pallas_call(
            kernel,
            out_shape=out_shape,
            in_specs=in_specs or [here] * len(args),
            out_specs=out_specs or jax.tree.map(lambda _: here, out_shape),
            scratch_shapes=list(scratch),
            compiler_params=pltpu.CompilerParams(vmem_limit_bytes=VMEM_BYTES),
            cost_estimate=pl.CostEstimate(flops=flops, bytes_accessed=moved, transcendentals=0),
        )(*args)

    return run


def extended(cells, sides, width):
    for axis, dim in sides:
        head = lax.slice_in_dim(cells, 0, width, axis=dim)
        tail = lax.slice_in_dim(cells, cells.shape[dim] - width, cells.shape[dim], axis=dim)
        cells = jnp.concatenate(
            [shifted(tail, axis, 1), cells, shifted(head, axis, -1)], axis=dim
        )
    return cells


def rims(inputs, extra):
    frames, rows, cols, channels = inputs[0].shape

    def piece(*shape):
        return jax.ShapeDtypeStruct((*shape, channels), inputs[0].dtype)

    halo, row, col, corner, *held = call(
        cut_kernel,
        (
            piece(extra, rows, cols),
            piece(frames + extra, cols),
            piece(frames + extra, rows),
            piece(frames + extra),
            *[jax.ShapeDtypeStruct(value.shape, value.dtype) for value in inputs],
        ),
        scratch=(pltpu.SemaphoreType.DMA((len(inputs) + 1,)),),
        in_specs=[pl.BlockSpec(memory_space=pltpu.HBM)] * len(inputs),
    )(*[pltpu.with_memory_space_constraint(value, pltpu.HBM) for value in inputs])
    halo = shifted(halo, "tm", -1)
    row = exchanged(row, "height", 1)
    corner = lax.ppermute(corner, ("height", "width"), [(i, 3 - i) for i in range(4)])
    col = exchanged(col, "width", 1)
    packed = call(pack_kernel, piece(extra, cols + rows + 1))(row, col, corner)
    tail = shifted(packed, "tm", -1)
    return held, (row, col, corner), (halo, tail)


def on_device(features, grad_out, mean_saved, rstd_saved, gain, bias, weight, future_cot):
    frames, rows, cols, channels = features.shape
    extra = weight.shape[0] - 1
    cells = rows * cols
    groups = mean_saved.shape[1]
    blocks = lax.axis_size("tm")
    taps = math.prod(weight.shape[:3])
    rows_out = taps * channels // blocks
    positions = cells * lax.axis_size("height") * lax.axis_size("width")
    grad_scale = 1.0 / math.sqrt(positions * frames * blocks)
    gain = gain.reshape(1, channels)
    bias = bias.reshape(1, channels)
    pair = paired()
    halves = in_halves(blocks, rows_out)
    f32, bf16 = jnp.float32, jnp.bfloat16
    work = 2 * taps * channels * channels * frames * cells
    early = frames - extra

    def shape(*dims, kind=f32):
        return jax.ShapeDtypeStruct((*dims, channels), kind)

    def window_shape(count):
        return jax.ShapeDtypeStruct((count, rows + 2, cols, 3 * channels), bf16)

    def stage_shape(count):
        return pltpu.VMEM((count, rows + 2, cols + 2 * LEAD, channels), f32)

    if pair:
        held, near_rims, (halo, tail) = rims(
            (grad_out, features, mean_saved, rstd_saved, gain, bias), extra
        )
        grad_out, features, mean_saved, rstd_saved, gain, bias = held
        late_sources = (halo, tail)

    act, last, params = call(
        act_kernel,
        (
            jax.ShapeDtypeStruct((channels, frames * cells), bf16),
            shape(extra, rows, cols, kind=bf16),
            shape(2 * frames + 2),
        ),
        flops=20 * frames * cells * channels,
        moved=4 * frames * cells * channels,
    )(features, mean_saved, rstd_saved, gain, bias)

    if pair:
        near_sources = (grad_out, *near_rims, last, params)
    else:
        axes = (("height", 1), ("width", 2))
        sides = ((0, 0), (0, 0), (LEAD - 1, LEAD - 1), (0, 0))
        padded = extended(grad_out, axes, 1)
        near_sources = (jnp.pad(padded, sides), jnp.pad(extended(last, axes, 1), sides))
        halo = shifted(grad_out[:extra], "tm", -1)
        late_sources = (jnp.pad(shifted(padded[:extra], "tm", -1), sides),)

    near_window, near_sum, act_window = call(
        functools.partial(near_kernel, grad_scale, pair, extra),
        (window_shape(frames), shape(taps * channels), window_shape(extra)),
        scratch=(stage_shape(frames),),
        flops=3 * work // 4,
        moved=4 * 1024 * 1024,
    )(act, *near_sources)

    if halves:
        sum_shapes = (
            shape(blocks, rows_out // 2),
            shape(blocks, rows_out // 2, kind=bf16),
        )
    else:
        sum_shapes = (shape(taps * channels),)
    sums = call(
        functools.partial(far_kernel, rows_out, grad_scale, halves, frames),
        sum_shapes,
        scratch=(pltpu.VMEM((taps * channels, channels), f32),),
        flops=work // 4,
        moved=4 * 1024 * 1024,
    )(act_window, near_sum, halo)

    if halves:
        weight_grad = reduced_share(*sums, rows_out)
    else:
        share = lax.psum_scatter(sums[0], "tm", scatter_dimension=0, tiled=True)
        weight_grad = lax.psum(share, ("height", "width"))

    scaled, before = [], []
    if early:
        value, local = call(
            early_kernel,
            (shape(early, rows, cols), shape(2 * frames)),
            flops=work * early // frames,
            moved=4 * 1024 * 1024,
        )(near_window, weight, features, params)
        scaled.append(value)
        before.append(local)
    value, local = call(
        functools.partial(late_kernel, pair, early),
        (shape(extra, rows, cols), shape(2 * frames)),
        scratch=(
            pltpu.VMEM(window_shape(extra).shape, bf16),
            stage_shape(extra),
        ),
        flops=work * extra // frames,
        moved=4 * 1024 * 1024,
    )(*late_sources, near_window, weight, future_cot, features, params, *before)
    scaled.append(value)

    if pair:
        parts = [local]
        parts.append(exchanged(local, "width", 1))
        parts.append(exchanged(local, "height", 1))
        parts.append(
            lax.ppermute(local, ("height", "width"), [(i, 3 - i) for i in range(4)])
        )
    else:
        parts = [lax.psum(local, ("height", "width"))]
    input_cot = call(
        functools.partial(final_kernel, groups, positions * (channels // groups), len(parts)),
        shape(frames, rows, cols, kind=bf16),
        flops=20 * frames * cells * channels,
        moved=10 * frames * cells * channels,
        out_specs=pl.BlockSpec(features.shape, lambda: (0, 0, 0, 0)),
    )(*parts, *scaled, features, grad_out, params)
    return (input_cot, weight_grad)


def solution(mesh):
    placed = (
        P("tm", "height", "width", None),
        P("tm", "height", "width", None),
        P("tm", None),
        P("tm", None),
        P(),
        P(),
        P(),
        P(None, "height", "width", None),
    )
    return jax.shard_map(
        on_device,
        mesh=mesh,
        in_specs=placed,
        out_specs=(P("tm", "height", "width", None), P("tm", None)),
        check_vma=False,
    )
```

```python
import functools
import math

import jax
import jax.numpy as jnp
from jax import lax
from jax.experimental import pallas as pl
from jax.experimental.pallas import tpu as pltpu
from jax.sharding import PartitionSpec as P


LEAD = 8
VMEM_BYTES = 12 * 1024 * 1024


def exchanged(value, axis, distance):
    count = lax.axis_size(axis)
    return lax.ppermute(value, axis, [(i, i ^ distance) for i in range(count)])


def shifted(value, axis, steps):
    count = lax.axis_size(axis)
    initial, last = (max(0, -steps), min(count, count - steps))
    return lax.ppermute(value, axis, [(source, source + steps) for source in range(initial, last)])


def power_of_two(count):
    return count & (count - 1) == 0


def paired():
    return lax.axis_size("height") == 2 and lax.axis_size("width") == 2


def in_halves(blocks, rows):
    return paired() and power_of_two(blocks) and blocks >= 8 and rows % 16 == 0


def tm_side(distance):
    return (lax.axis_index("tm") // distance) % 2


def first_kernel(mine_ref, got_ref, low_near, low_far, high_near, high_far):
    half = mine_ref.shape[0] // 2
    near_side, next_side = tm_side(1), tm_side(2)

    def block(at):
        return mine_ref[at] + got_ref[at].astype(jnp.float32)

    for i in range(low_near.shape[0]):
        low_near[i] = block(2 * i + near_side)
        low_far[i] = block(2 * i + 1 - near_side).astype(low_far.dtype)
    for i in range(high_near.shape[0]):
        at = half + 4 * (i // 2) + i % 2
        high_near[i] = block(at + 2 * next_side)
        high_far[i] = block(at + 2 * (1 - next_side)).astype(high_far.dtype)


def second_kernel(low_ref, low_got_ref, high_ref, high_got_ref, *outs):
    low_near, low_far, high_near, high_far = outs

    def halve(value_ref, got_ref, near_ref, far_ref, side):
        for i in range(near_ref.shape[0]):
            at = 2 * i + side
            near_ref[i] = value_ref[at] + got_ref[at].astype(jnp.float32)
            at = 2 * i + 1 - side
            value = value_ref[at] + got_ref[at].astype(jnp.float32)
            far_ref[i] = value.astype(far_ref.dtype)

    halve(low_ref, low_got_ref, low_near, low_far, tm_side(2))
    halve(high_ref, high_got_ref, high_near, high_far, tm_side(1))


def split_kernel(distance, *refs):
    *parts, near_ref, far_ref = refs
    blocks = [
        (value_ref, got_ref, at)
        for value_ref, got_ref in zip(parts[::2], parts[1::2])
        for at in range(value_ref.shape[0])
    ]

    def block(i):
        value_ref, got_ref, at = blocks[i]
        return value_ref[at] + got_ref[at].astype(jnp.float32)

    for which in range(2):

        @pl.when(tm_side(distance) == which)
        def _():
            for i in range(near_ref.shape[0]):
                near_ref[i] = block(2 * i + which)
                far_ref[i] = block(2 * i + 1 - which).astype(far_ref.dtype)


def total_kernel(own_ref, got_ref, below_ref, below_got_ref, out_ref):
    mine = own_ref[...] + got_ref[...].astype(jnp.float32)
    out_ref[...] = mine + (below_ref[...] + below_got_ref[...].astype(jnp.float32))


def whole_kernel(own_ref, beside_ref, out_hbm, sems):
    half = own_ref.shape[1]
    side = lax.axis_index("width")
    copies = []
    for i, (ref, place) in enumerate(((own_ref, side), (beside_ref, 1 - side))):
        rows = pl.ds(pl.multiple_of(place * half, 8), half)
        copies.append(pltpu.make_async_copy(ref.at[0], out_hbm.at[rows, :], sems.at[i]))
    for copy in copies:
        copy.start()
    for copy in copies:
        copy.wait()


def reduced_share(mine, theirs, rows):
    blocks, half, channels = mine.shape
    f32, wire = jnp.float32, jnp.bfloat16

    def both(count):
        return tuple(jax.ShapeDtypeStruct((count, half, channels), kind) for kind in (f32, wire))

    got = exchanged(theirs, "width", 1)
    low, low_far, high, high_far = call(
        first_kernel, (*both(blocks // 4), *both(blocks // 4))
    )(mine, got)
    low_got = exchanged(low_far, "tm", 1)
    high_got = exchanged(high_far, "tm", 2)
    low, low_far, high, high_far = call(
        second_kernel, (*both(blocks // 8), *both(blocks // 8))
    )(low, low_got, high, high_got)
    low_got = exchanged(low_far, "tm", 2)
    high_got = exchanged(high_far, "tm", 1)
    parts = (low, low_got, high, high_got)
    distance = 4
    while distance < blocks:
        near, far = call(
            functools.partial(split_kernel, distance), both(blocks // distance // 2)
        )(*parts)
        parts = (near, exchanged(far, "tm", distance))
        distance *= 2
    own, got = parts
    below = exchanged(own, "height", 1)
    below_got = exchanged(got, "height", 1)
    total = call(total_kernel, both(1)[0])(own, got, below, below_got)
    beside = exchanged(total, "width", 1)
    return call(
        whole_kernel,
        jax.ShapeDtypeStruct((rows, channels), f32),
        scratch=(pltpu.SemaphoreType.DMA((2,)),),
        out_specs=pl.BlockSpec(memory_space=pltpu.HBM),
    )(total, beside)


def group_matrix(rows, cols, row_width, col_width):
    row = lax.broadcasted_iota(jnp.int32, (rows, cols), 0) // row_width
    col = lax.broadcasted_iota(jnp.int32, (rows, cols), 1) // col_width
    return (row == col).astype(jnp.float32)


def exact_dot(left, right):
    return lax.dot_general(
        left,
        right,
        (((1,), (0,)), ((), ())),
        precision=lax.Precision.HIGHEST,
        preferred_element_type=jnp.float32,
    )


def per_channel(value, channels):
    groups = value.shape[1]
    return exact_dot(value, group_matrix(groups, channels, 1, channels // groups))


def cut_kernel(*refs):
    sources, (halo_ref, row_ref, col_ref, corner_ref), held, sems = (
        refs[:6],
        refs[6:10],
        refs[10:-1],
        refs[-1],
    )
    extra = halo_ref.shape[0]
    pairs = [(sources[0].at[0:extra], halo_ref), *zip(sources, held)]
    copies = [
        pltpu.make_async_copy(source, target, sems.at[i])
        for i, (source, target) in enumerate(pairs)
    ]
    for copy in copies:
        copy.start()
    for copy in copies:
        copy.wait()
    grad_ref, features_ref = held[:2]
    frames, rows, cols, _ = grad_ref.shape
    row_at = (1 - lax.axis_index("height")) * (rows - 1)
    taken = [grad_ref.at[f] for f in range(frames)]
    taken += [features_ref.at[f] for f in range(frames - extra, frames)]

    def columns(at):
        corners = []
        for i, ref in enumerate(taken):
            col_ref[i] = ref[...].astype(jnp.float32)[:, at].astype(jnp.bfloat16)
            corners.append(ref[row_at].astype(jnp.float32)[at : at + 1])
        corner_ref[...] = jnp.concatenate(corners, axis=0).astype(jnp.bfloat16)

    for i, ref in enumerate(taken):
        row_ref[i] = ref[row_at]

    @pl.when(lax.axis_index("width") == 0)
    def _():
        columns(cols - 1)

    @pl.when(lax.axis_index("width") == 1)
    def _():
        columns(0)


def pack_kernel(row_ref, col_ref, corner_ref, tail_ref):
    cols, rows = row_ref.shape[1], col_ref.shape[1]
    for f in range(tail_ref.shape[0]):
        tail_ref[f, 0:cols] = row_ref[f]
        tail_ref[f, cols : cols + rows] = col_ref[f]
        tail_ref[f, cols + rows :] = corner_ref[f : f + 1]


def activation(value, params, frames, t):
    centred = (value - params[t : t + 1]) * params[frames + t : frames + t + 1]
    pre_act = centred * params[2 * frames : 2 * frames + 1]
    pre_act = pre_act + params[2 * frames + 1 : 2 * frames + 2]
    sig = jax.nn.sigmoid(pre_act)
    return centred, pre_act, sig


def act_kernel(
    features_ref, mean_ref, rstd_ref, gain_ref, bias_ref, act_ref, last_ref, params_ref
):
    frames, rows, cols, channels = features_ref.shape
    cells = rows * cols
    mean = per_channel(mean_ref[...], channels)
    rstd = per_channel(rstd_ref[...], channels)
    params = jnp.concatenate([mean, rstd, gain_ref[...], bias_ref[...]], axis=0)
    params_ref[...] = params
    for t in range(frames):
        value = features_ref[t].astype(jnp.float32).reshape(cells, channels)
        _, pre_act, sig = activation(value, params, frames, t)
        act = (pre_act * sig).astype(jnp.bfloat16)
        act_ref[:, t * cells : (t + 1) * cells] = act.T
        later = t - (frames - last_ref.shape[0])
        if later >= 0:
            last_ref[later] = act.reshape(rows, cols, channels)


def fill_pair(stage_ref, inner_ref, row_of, col_of, corner_of):
    total, rows, cols, channels = inner_ref.shape
    row_side = lax.axis_index("height")
    col_side = lax.axis_index("width")
    rim_row = (1 - row_side) * (rows + 1)
    for f in range(total):
        zeros = jnp.zeros((rows + 2, LEAD, channels), jnp.float32)
        stage_ref[f, :, 0:LEAD, :] = zeros
        stage_ref[f, :, LEAD + cols :, :] = zeros
        empty = jnp.zeros((cols, channels), jnp.float32)
        stage_ref[f, 0, LEAD : LEAD + cols, :] = empty
        stage_ref[f, rows + 1, LEAD : LEAD + cols, :] = empty
        stage_ref[f, 1 : rows + 1, LEAD : LEAD + cols, :] = inner_ref[f].astype(jnp.float32)
        stage_ref[f, rim_row, LEAD : LEAD + cols, :] = row_of(f).astype(jnp.float32)

    def fill_columns(at):
        for f in range(total):
            column = col_of(f).astype(jnp.float32)
            for r in range(rows):
                stage_ref[f, r + 1, at : at + 1, :] = column[r : r + 1]
            stage_ref[f, rim_row, at : at + 1, :] = corner_of(f).astype(jnp.float32)

    @pl.when(col_side == 1)
    def _():
        fill_columns(LEAD - 1)

    @pl.when(col_side == 0)
    def _():
        fill_columns(LEAD + cols)


def widen(stage_ref, window_ref):
    total, _, cols, wide = window_ref.shape
    channels = wide // 3

    def one(f, carry):
        for e in range(3):
            at = LEAD - 1 + e
            window_ref[f, :, :, e * channels : (e + 1) * channels] = stage_ref[
                f, :, at : at + cols, :
            ].astype(jnp.bfloat16)
        return carry

    lax.fori_loop(0, total, one, 0)


def tap_sums(act_ref, scale, pairs, window_of, shape, lag_t, add):
    rows, cols, channels = shape
    cells = rows * cols
    for lag_h in range(3):
        acc = None
        for t, f in pairs:
            window = window_of(f)[2 - lag_h : 2 - lag_h + rows]
            term = lax.dot_general(
                act_ref[:, t * cells : (t + 1) * cells],
                window.reshape(cells, window.shape[-1]),
                (((1,), (0,)), ((), ())),
                preferred_element_type=jnp.float32,
            )
            acc = term if acc is None else acc + term
        for lag_w in range(3):
            e = 2 - lag_w
            at = ((lag_t * 3 + lag_h) * 3 + lag_w) * channels
            if acc is None:
                value = jnp.zeros((channels, channels), jnp.float32)
            else:
                value = scale * acc[:, e * channels : (e + 1) * channels]
            add(at, value)


def near_kernel(scale, pair, extra, act_ref, *refs):
    sources, (window_ref, sum_ref, act_window_ref, stage_ref) = refs[:-4], refs[-4:]
    frames, rows_ext, cols, wide = window_ref.shape
    shape = (rows_ext - 2, cols, wide // 3)
    if pair:
        grad_ref, row_ref, col_ref, corner_ref, last_ref, params_ref = sources
        params = params_ref[...]

        def rim_act(value, f):
            value = value.astype(jnp.float32)
            _, pre_act, sig = activation(value, params, frames, frames - extra + f)
            return (pre_act * sig).astype(jnp.bfloat16)

        fill_pair(
            stage_ref,
            grad_ref,
            lambda f: row_ref[f],
            lambda f: col_ref[f],
            lambda f: corner_ref[f : f + 1],
        )
        widen(stage_ref, window_ref)
        fill_pair(
            stage_ref,
            last_ref,
            lambda f: rim_act(row_ref[frames + f], f),
            lambda f: rim_act(col_ref[frames + f], f),
            lambda f: rim_act(corner_ref[frames + f : frames + f + 1], f),
        )
        widen(stage_ref, act_window_ref)
    else:
        stage_ref[...] = sources[0][...].astype(jnp.float32)
        widen(stage_ref, window_ref)
        stage_ref[:extra] = sources[1][...].astype(jnp.float32)
        widen(stage_ref, act_window_ref)

    def put(at, value):
        sum_ref[at : at + value.shape[0], :] = value

    for lag_t in range(extra + 1):
        ahead = extra - lag_t
        pairs = [(t, t + ahead) for t in range(frames) if t + ahead < frames]
        tap_sums(act_ref, scale, pairs, lambda f: window_ref.at[f], shape, lag_t, put)


def far_kernel(rows_out, scale, halves, frames, act_window_ref, near_sum_ref, halo_ref, *refs):
    outs, sum_ref = refs[:-1], refs[-1]
    extra, rows, cols, channels = halo_ref.shape
    cells = rows * cols
    flipped = [halo_ref[f].reshape(cells, channels).T for f in range(extra)]
    for lag_t in range(extra):
        ahead = extra - lag_t
        pairs = [(t, t + ahead - frames) for t in range(frames) if t + ahead >= frames]
        for lag_h in range(3):
            acc = None
            for t, f in pairs:
                window = act_window_ref[t - (frames - extra), lag_h : lag_h + rows]
                term = lax.dot_general(
                    flipped[f],
                    window.reshape(cells, 3 * channels),
                    (((1,), (0,)), ((), ())),
                    preferred_element_type=jnp.float32,
                )
                acc = term if acc is None else acc + term
            for lag_w in range(3):
                at = ((lag_t * 3 + lag_h) * 3 + lag_w) * channels
                value = scale * acc[:, lag_w * channels : (lag_w + 1) * channels].T
                sum_ref[at : at + channels, :] = near_sum_ref[at : at + channels, :] + value
    done = extra * 9 * channels
    sum_ref[done:, :] = near_sum_ref[done:, :]
    if not halves:
        outs[0][...] = sum_ref[...]
        return
    mine_ref, theirs_ref = outs
    col_side = lax.axis_index("width")
    half = rows_out // 2

    def place(low_ref, high_ref):
        for block in range(mine_ref.shape[0]):
            at = block * rows_out
            low_ref[block] = sum_ref[at : at + half, :].astype(low_ref.dtype)
            high_ref[block] = sum_ref[at + half : at + rows_out, :].astype(high_ref.dtype)

    @pl.when(col_side == 0)
    def _():
        place(mine_ref, theirs_ref)

    @pl.when(col_side == 1)
    def _():
        place(theirs_ref, mine_ref)


def conv_frames(window_of, weight_ref, future_ref, features_ref, params, span, scaled_ref, put):
    frames, rows, cols, channels = features_ref.shape
    cells = rows * cols
    extra = weight_ref.shape[0] - 1
    gain = params[2 * frames : 2 * frames + 1]
    is_last = lax.axis_index("tm") == lax.axis_size("tm") - 1
    for t in span:
        acc = None
        for lag_t in range(extra + 1):
            for lag_h in range(3):
                window = window_of(t + extra - lag_t)[2 - lag_h : 2 - lag_h + rows]
                taps = jnp.concatenate(
                    [weight_ref[lag_t, lag_h, 2 - e] for e in range(3)], axis=1
                )
                term = lax.dot_general(
                    window.reshape(cells, 3 * channels),
                    taps,
                    (((1,), (1,)), ((), ())),
                    preferred_element_type=jnp.float32,
                )
                acc = term if acc is None else acc + term
        later = t - (frames - extra)
        if later >= 0:
            tail = future_ref[later].astype(jnp.float32).reshape(cells, channels)
            acc = acc + jnp.where(is_last, tail, jnp.zeros_like(tail))
        value = features_ref[t].astype(jnp.float32).reshape(cells, channels)
        centred, pre_act, sig = activation(value, params, frames, t)
        scaled = acc * sig * (1.0 + pre_act * (1.0 - sig)) * gain
        scaled_ref[t - span[0]] = scaled.reshape(rows, cols, channels)
        put(t, jnp.sum(scaled, axis=0, keepdims=True))
        put(frames + t, jnp.sum(scaled * centred, axis=0, keepdims=True))


def early_kernel(near_ref, weight_ref, features_ref, params_ref, scaled_ref, sums_ref):
    sums_ref[...] = jnp.zeros_like(sums_ref)

    def put(at, value):
        sums_ref[at : at + 1, :] = value

    conv_frames(
        lambda f: near_ref.at[f],
        weight_ref,
        None,
        features_ref,
        params_ref[...],
        range(scaled_ref.shape[0]),
        scaled_ref,
        put,
    )


def late_kernel(pair, early, *refs):
    count = 2 if pair else 1
    sources = refs[:count]
    near_ref, weight_ref, future_ref, features_ref, params_ref = refs[count : count + 5]
    before, (scaled_ref, sums_ref, window_ref, stage_ref) = refs[count + 5 : -4], refs[-4:]
    frames, rows, cols, _ = features_ref.shape
    if pair:
        halo_ref, tail_ref = sources
        fill_pair(
            stage_ref,
            halo_ref,
            lambda f: tail_ref[f, 0:cols],
            lambda f: tail_ref[f, cols : cols + rows],
            lambda f: tail_ref[f, cols + rows : cols + rows + 1],
        )
    else:
        stage_ref[...] = sources[0][...].astype(jnp.float32)
    widen(stage_ref, window_ref)
    if before:
        sums_ref[...] = before[0][...]

    def put(at, value):
        sums_ref[at : at + 1, :] = value

    conv_frames(
        lambda f: near_ref.at[f] if f < frames else window_ref.at[f - frames],
        weight_ref,
        future_ref,
        features_ref,
        params_ref[...],
        range(early, frames),
        scaled_ref,
        put,
    )


def final_kernel(groups, count, terms, *refs):
    parts, scaled_refs, (features_ref, grad_ref, params_ref, out_ref) = (
        refs[:terms],
        refs[terms:-4],
        refs[-4:],
    )
    scaled = [ref.at[t] for ref in scaled_refs for t in range(ref.shape[0])]
    frames, _, _, channels = features_ref.shape
    mean = params_ref[0:frames]
    rstd = params_ref[frames : 2 * frames]
    total = parts[0][...]
    for part in parts[1:]:
        total = total + part[...]
    width = channels // groups
    means = exact_dot(total, group_matrix(channels, channels, width, width)) / count
    for t in range(frames):
        value = features_ref[t].astype(jnp.float32)
        centred = (value - mean[t : t + 1]) * rstd[t : t + 1]
        first = means[t : t + 1]
        second = means[frames + t : frames + t + 1]
        corrected = rstd[t : t + 1] * (scaled[t][...] - first - centred * second)
        out_ref[t] = (grad_ref[t].astype(jnp.float32) + corrected).astype(jnp.bfloat16)


def call(kernel, out_shape, scratch=(), flops=0, moved=0, in_specs=None, out_specs=None):
    here = pl.BlockSpec(memory_space=pltpu.VMEM)

    def run(*args):
        return pl.pallas_call(
            kernel,
            out_shape=out_shape,
            in_specs=in_specs or [here] * len(args),
            out_specs=out_specs or jax.tree.map(lambda _: here, out_shape),
            scratch_shapes=list(scratch),
            compiler_params=pltpu.CompilerParams(vmem_limit_bytes=VMEM_BYTES),
            cost_estimate=pl.CostEstimate(flops=flops, bytes_accessed=moved, transcendentals=0),
        )(*args)

    return run


def extended(cells, sides, width):
    for axis, dim in sides:
        head = lax.slice_in_dim(cells, 0, width, axis=dim)
        tail = lax.slice_in_dim(cells, cells.shape[dim] - width, cells.shape[dim], axis=dim)
        cells = jnp.concatenate(
            [shifted(tail, axis, 1), cells, shifted(head, axis, -1)], axis=dim
        )
    return cells


def rims(inputs, extra):
    frames, rows, cols, channels = inputs[0].shape

    def piece(*shape):
        return jax.ShapeDtypeStruct((*shape, channels), inputs[0].dtype)

    halo, row, col, corner, *held = call(
        cut_kernel,
        (
            piece(extra, rows, cols),
            piece(frames + extra, cols),
            piece(frames + extra, rows),
            piece(frames + extra),
            *[jax.ShapeDtypeStruct(value.shape, value.dtype) for value in inputs],
        ),
        scratch=(pltpu.SemaphoreType.DMA((len(inputs) + 1,)),),
        in_specs=[pl.BlockSpec(memory_space=pltpu.HBM)] * len(inputs),
    )(*[pltpu.with_memory_space_constraint(value, pltpu.HBM) for value in inputs])
    halo = shifted(halo, "tm", -1)
    row = exchanged(row, "height", 1)
    corner = lax.ppermute(corner, ("height", "width"), [(i, 3 - i) for i in range(4)])
    col = exchanged(col, "width", 1)
    packed = call(pack_kernel, piece(extra, cols + rows + 1))(row, col, corner)
    tail = shifted(packed, "tm", -1)
    return held, (row, col, corner), (halo, tail)


def on_device(features, grad_out, mean_saved, rstd_saved, gain, bias, weight, future_cot):
    frames, rows, cols, channels = features.shape
    extra = weight.shape[0] - 1
    cells = rows * cols
    groups = mean_saved.shape[1]
    blocks = lax.axis_size("tm")
    taps = math.prod(weight.shape[:3])
    rows_out = taps * channels // blocks
    positions = cells * lax.axis_size("height") * lax.axis_size("width")
    grad_scale = 1.0 / math.sqrt(positions * frames * blocks)
    gain = gain.reshape(1, channels)
    bias = bias.reshape(1, channels)
    pair = paired()
    halves = in_halves(blocks, rows_out)
    f32, bf16 = jnp.float32, jnp.bfloat16
    work = 2 * taps * channels * channels * frames * cells
    early = frames - extra

    def shape(*dims, kind=f32):
        return jax.ShapeDtypeStruct((*dims, channels), kind)

    def window_shape(count):
        return jax.ShapeDtypeStruct((count, rows + 2, cols, 3 * channels), bf16)

    def stage_shape(count):
        return pltpu.VMEM((count, rows + 2, cols + 2 * LEAD, channels), f32)

    if pair:
        held, near_rims, (halo, tail) = rims(
            (grad_out, features, mean_saved, rstd_saved, gain, bias), extra
        )
        grad_out, features, mean_saved, rstd_saved, gain, bias = held
        late_sources = (halo, tail)

    act, last, params = call(
        act_kernel,
        (
            jax.ShapeDtypeStruct((channels, frames * cells), bf16),
            shape(extra, rows, cols, kind=bf16),
            shape(2 * frames + 2),
        ),
        flops=20 * frames * cells * channels,
        moved=4 * frames * cells * channels,
    )(features, mean_saved, rstd_saved, gain, bias)

    if pair:
        near_sources = (grad_out, *near_rims, last, params)
    else:
        axes = (("height", 1), ("width", 2))
        sides = ((0, 0), (0, 0), (LEAD - 1, LEAD - 1), (0, 0))
        padded = extended(grad_out, axes, 1)
        near_sources = (jnp.pad(padded, sides), jnp.pad(extended(last, axes, 1), sides))
        halo = shifted(grad_out[:extra], "tm", -1)
        late_sources = (jnp.pad(shifted(padded[:extra], "tm", -1), sides),)

    near_window, near_sum, act_window = call(
        functools.partial(near_kernel, grad_scale, pair, extra),
        (window_shape(frames), shape(taps * channels), window_shape(extra)),
        scratch=(stage_shape(frames),),
        flops=3 * work // 4,
        moved=4 * 1024 * 1024,
    )(act, *near_sources)

    if halves:
        sum_shapes = (
            shape(blocks, rows_out // 2),
            shape(blocks, rows_out // 2, kind=bf16),
        )
    else:
        sum_shapes = (shape(taps * channels),)
    sums = call(
        functools.partial(far_kernel, rows_out, grad_scale, halves, frames),
        sum_shapes,
        scratch=(pltpu.VMEM((taps * channels, channels), f32),),
        flops=work // 4,
        moved=4 * 1024 * 1024,
    )(act_window, near_sum, halo)

    if halves:
        weight_grad = reduced_share(*sums, rows_out)
    else:
        share = lax.psum_scatter(sums[0], "tm", scatter_dimension=0, tiled=True)
        weight_grad = lax.psum(share, ("height", "width"))

    scaled, before = [], []
    if early:
        value, local = call(
            early_kernel,
            (shape(early, rows, cols), shape(2 * frames)),
            flops=work * early // frames,
            moved=4 * 1024 * 1024,
        )(near_window, weight, features, params)
        scaled.append(value)
        before.append(local)
    value, local = call(
        functools.partial(late_kernel, pair, early),
        (shape(extra, rows, cols), shape(2 * frames)),
        scratch=(
            pltpu.VMEM(window_shape(extra).shape, bf16),
            stage_shape(extra),
        ),
        flops=work * extra // frames,
        moved=4 * 1024 * 1024,
    )(*late_sources, near_window, weight, future_cot, features, params, *before)
    scaled.append(value)

    if pair:
        parts = [local]
        parts.append(exchanged(local, "width", 1))
        parts.append(exchanged(local, "height", 1))
        parts.append(
            lax.ppermute(local, ("height", "width"), [(i, 3 - i) for i in range(4)])
        )
    else:
        parts = [lax.psum(local, ("height", "width"))]
    input_cot = call(
        functools.partial(final_kernel, groups, positions * (channels // groups), len(parts)),
        shape(frames, rows, cols, kind=bf16),
        flops=20 * frames * cells * channels,
        moved=10 * frames * cells * channels,
        out_specs=pl.BlockSpec(features.shape, lambda: (0, 0, 0, 0)),
    )(*parts, *scaled, features, grad_out, params)
    return (input_cot, weight_grad)


def solution(mesh):
    placed = (
        P("tm", "height", "width", None),
        P("tm", "height", "width", None),
        P("tm", None),
        P("tm", None),
        P(),
        P(),
        P(),
        P(None, "height", "width", None),
    )
    return jax.shard_map(
        on_device,
        mesh=mesh,
        in_specs=placed,
        out_specs=(P("tm", "height", "width", None), P("tm", None)),
        check_vma=False,
    )
```
